32 devices in a mesh: groups: 2 (over y), cells: 4 (over z), nodes: 2 (over x), sub: 2 (over core).
Axes of the slice: x: 2, y: 2, z: 4, core: 2. Of those that a mesh axis runs over, the one named last changes fastest.
Arguments:
- adjoint_start: float32 [4, 5, 16384], P('nodes', None, ('groups', 'cells', 'sub')), parts along dimension 2, may hold values from -6 to 6
- adjoint_rhs: float32 [4, 5, 16384], P('nodes', None, ('groups', 'cells', 'sub')), parts along dimension 2, may hold values from -6 to 6
- off_blocks: bfloat16 [4, 6, 25, 16384], P('nodes', None, None, ('groups', 'cells', 'sub')), parts along dimension 3, may hold values from -0.5 to 0.5
- diag_inverse: float32 [4, 25, 16384], P('nodes', None, ('groups', 'cells', 'sub')), parts along dimension 2, may hold values from -2.4 to 2.4
- neighbours: int32 [6, 8192], P(None, ('cells', 'sub')), may hold values from -1 to 8191, as said below
- node_weights: float32 [4], P('nodes'), may hold values from 0.05 to 0.5
- sens_blocks: bfloat16 [4, 15, 16384], P('nodes', None, ('groups', 'cells', 'sub')), parts along dimension 2, may hold values from -1.796875 to 1.796875
- cell_points: float32 [3, 8192], P(None, ('cells', 'sub')), may hold values from 0 to 1
- base_points: float32 [3, 4096], replicated, may hold values from 0 to 1
- ffd_index: int32 [4096, 8], replicated, may hold values from 0 to 511
- ffd_weight: float32 [4096, 8], replicated, may hold values from 0 to 1
Outputs:
- adjoint: float32 [4, 5, 16384], P('nodes', None, ('groups', 'cells', 'sub')), parts along dimension 2
- control_grad: float32 [6, 512], P('groups'), parts along dimension 0
The draws below stay inside these ranges and needn't reach their ends.
There are 2 independent parts, one for each index of `groups`. The reference program is written for one: setup_inputs(seed, part) draws one part's arguments, and reference() takes and returns one part's arrays. A program takes and returns all parts, laid end to end along the dimension named above; an argument that names none is the same for every part. Nothing has to cross between parts.
Inputs may be any that keep to these rules, and one draw needn't show every extreme that they name: `neighbours`: each entry is -1 (no neighbour) or the index of a cell at most 1024 away from the cell; the distance 1024 occurs.
All inputs are finite; a program needn't handle non-finite values.
Results may differ from the reference program's by a relative error of at most 0.0003.
Values sent between devices are 32-bit elements; how exact they have to be, the bound alone decides.
A program may use at most 64 MiB of HBM per device.

```python
import math
import jax
import jax.numpy as jnp
from jax import lax

REACH = 1024
NODES = 4
NCELLS = 8192
FACES = 6
SWEEPS = 2
BASE = 4096
FFD = 512


def draw_neighbours(key, part):
    key_dist = jax.random.fold_in(key, 11)
    key_sign = jax.random.fold_in(key, 12)
    key_pad = jax.random.fold_in(key, 13)
    distance = jax.random.randint(key_dist, (FACES, NCELLS), 1, REACH + 1)
    upward = jax.random.randint(key_sign, (FACES, NCELLS), 0, 2)
    offset = jnp.where(upward == 1, distance, -distance)
    target = jnp.arange(NCELLS, dtype=jnp.int32)[None, :] + offset
    padded = jax.random.randint(key_pad, (FACES, NCELLS), 0, 6) == 0
    inside = (target >= 0) & (target < NCELLS)
    result = jnp.where(inside & jnp.logical_not(padded), target, -1).astype(jnp.int32)
    return result.at[0, REACH].set(0)


def touch_ends(values, rng, least, high):
    index_at = [jax.random.randint(jax.random.fold_in(rng, axis), (), 0, length) for axis, length in enumerate(values.shape)]
    main_axis = values.shape.index(max(values.shape))
    neighbour = index_at[:main_axis] + [(index_at[main_axis] + 1) % values.shape[main_axis]] + index_at[main_axis + 1:]
    return values.at[tuple(index_at)].set(least).at[tuple(neighbour)].set(high)


def block_scale(rng, dims, split, low, largest):
    level = 1.0
    for position, shards_of in split:
        steps = jax.random.uniform(jax.random.fold_in(jax.random.fold_in(rng, 6), position), (shards_of,), jnp.float32, low / len(split), largest / len(split))
        level = level * jnp.repeat(jnp.exp(steps), dims[position] // shards_of).reshape((-1,) + (1,) * (len(dims) - 1 - position))
    return level


def centred(stream_key, extent, scale, bound, cuts=(), kind=jnp.bfloat16):
    loudness = block_scale(stream_key, extent, cuts, -0.22, 0.18) if cuts else 1.0
    drawn = jax.random.normal(stream_key, extent, jnp.float32) * scale * loudness
    return jnp.minimum(jnp.maximum(drawn, -bound), bound).astype(kind)


def setup_inputs(seed: int = 0, part: int = 0) -> dict:
    key_of = jax.random.split(jax.random.key(seed), 12)
    part_splits = jax.random.split(jax.random.fold_in(key_of[11], part), 12)
    return {
        "adjoint_start": centred(part_splits[0], (NODES, 5, NCELLS), 1.0, 6.0, ((0, 2), (2, 8)), jnp.float32),
        "adjoint_rhs": centred(part_splits[1], (NODES, 5, NCELLS), 1.0, 6.0, ((0, 2), (2, 8)), jnp.float32),
        "off_blocks": centred(part_splits[2], (NODES, FACES, 25, NCELLS), 0.08, 0.5, ((0, 2), (3, 8))),
        "diag_inverse": centred(part_splits[3], (NODES, 25, NCELLS), 0.4, 2.4, ((0, 2), (2, 8)), jnp.float32),
        "neighbours": draw_neighbours(jax.random.fold_in(key_of[11], 71), part),
        "node_weights": jnp.clip(jnp.exp(math.log(0.5) - 2.3025851 * jax.random.uniform(key_of[5], (NODES,), jnp.float32) ** block_scale(key_of[5], (NODES,), ((0, 2),), -0.2, 0.2)), 0.05, 0.5),
        "sens_blocks": centred(part_splits[6], (NODES, 15, NCELLS), 0.3, 1.796875, ((0, 2), (2, 8))),
        "cell_points": jnp.clip(1.0 * jax.random.uniform(key_of[7], (3, NCELLS), jnp.float32) ** block_scale(key_of[7], (3, NCELLS), ((1, 8),), -0.2, 0.2), 0.0, 1.0),
        "base_points": jnp.clip(jax.random.uniform(key_of[8], (3, BASE), jnp.float32, 0.0, 1.0), 0.0, 1.0),
        "ffd_index": touch_ends(jax.random.randint(key_of[9], (BASE, 8), 0, FFD), jax.random.fold_in(key_of[9], 1), 0, FFD - 1).astype(jnp.int32),
        "ffd_weight": jnp.clip(jax.random.uniform(key_of[10], (BASE, 8), jnp.float32, 0.0, 1.0), 0.0, 1.0),
    }


support_radius = 0.3

def relax(adjoint, adjoint_rhs, off_blocks, diag_inverse, neighbours):
    present = neighbours >= 0
    index_safe = jnp.where(present, neighbours, 0)
    coupled = jnp.zeros(adjoint.shape, jnp.float32)
    node_count = adjoint.shape[0]
    for face_slot in range(FACES):
        beside = jnp.where(present[face_slot][None, None, :], adjoint[:, :, index_safe[face_slot]], 0.0)
        coupling = off_blocks[:, face_slot].astype(jnp.float32).reshape(node_count, 5, 5, -1)
        coupled = coupled + lax.optimization_barrier(jnp.sum(coupling * beside[:, None], axis=2))
    inverse = diag_inverse.reshape(node_count, 5, 5, -1)
    return lax.optimization_barrier(jnp.sum(inverse * (adjoint_rhs - coupled)[:, None], axis=2))

def kernel_sum(sensitivity, points, base):
    squared = jnp.zeros((points.shape[1], base.shape[1]), jnp.float32)
    for axis_slot in range(3):
        squared = squared + (points[axis_slot][:, None] - base[axis_slot][None, :]) ** 2
    ratio = jnp.sqrt(squared) / support_radius
    kernel = jnp.maximum(1.0 - ratio, 0.0) ** 4 * (4.0 * ratio + 1.0)
    return jnp.dot(sensitivity, kernel, precision=lax.Precision.HIGHEST, preferred_element_type=jnp.float32)

def lattice_matrix(lattice_index, lattice_weight, columns):
    matches = lattice_index[:, :, None] == jnp.arange(columns, dtype=jnp.int32)[None, None, :]
    return lax.optimization_barrier(jnp.sum(jnp.where(matches, lattice_weight[:, :, None], 0.0), axis=1))

def reference(adjoint_start, adjoint_rhs, off_blocks, diag_inverse, neighbours, node_weights, sens_blocks, cell_points, base_points, ffd_index, ffd_weight):
    adjoint = adjoint_start
    for sweep_step in range(SWEEPS):
        adjoint = relax(adjoint, adjoint_rhs, off_blocks, diag_inverse, neighbours)
    derive = sens_blocks.astype(jnp.float32).reshape(adjoint.shape[0], 5, 3, -1)
    per_node = lax.optimization_barrier(jnp.sum(adjoint[:, :, None] * derive, axis=1))
    sensitivity = lax.optimization_barrier(jnp.sum(node_weights[:, None, None] * per_node, axis=0))
    cell_block = min(4096, NCELLS)

    def add_block(block_index, carry):
        sens_part = lax.dynamic_slice_in_dim(sensitivity, block_index * cell_block, cell_block, 1)
        point_part = lax.dynamic_slice_in_dim(cell_points, block_index * cell_block, cell_block, 1)
        return carry + kernel_sum(sens_part, point_part, base_points)
    base_grad = lax.fori_loop(0, NCELLS // cell_block, add_block, jnp.zeros((3, BASE), jnp.float32))
    base_grad = base_grad / jnp.sqrt(jnp.float32(NCELLS))
    lattice = lattice_matrix(ffd_index, ffd_weight, FFD)
    control_grad = jnp.dot(base_grad, lattice, precision=lax.Precision.HIGHEST, preferred_element_type=jnp.float32)
    return (adjoint, control_grad)
```

```python
import functools

import jax
import jax.numpy as jnp
from jax import lax
from jax.experimental import pallas as pl
from jax.experimental.pallas import tpu as pltpu
from jax.sharding import PartitionSpec as P

SWEEPS = 2
FFD = 512
LANES = 128
ROWS = 8
PIECE = 64

support_radius = 0.3
MESH = pl.DeviceIdType.MESH


def split2(x):
    hi = x.astype(jnp.bfloat16)
    return hi, (x - hi.astype(jnp.float32)).astype(jnp.bfloat16)


def split3(x):
    one = x.astype(jnp.bfloat16).astype(jnp.float32)
    two = (x - one).astype(jnp.bfloat16).astype(jnp.float32)
    return one, two, (x - one) - two


def kernel(
    scale,
    weight_hbm,
    adj_hbm,
    point_hbm,
    nb_hbm,
    base_hbm,
    off_hbm,
    rhs_hbm,
    inv_hbm,
    sens_hbm,
    ffd_index_hbm,
    ffd_weight_hbm,
    out_ref,
    grad_ref,
    weight_ref,
    point_ref,
    nb_ref,
    base_ref,
    off_ref,
    rhs_ref,
    inv_ref,
    sens_ref,
    ffd_index_ref,
    ffd_weight_ref,
    wide,
    rel_ref,
    lane_ref,
    points,
    cell_rows,
    cell_feat,
    base_feat,
    k_hi,
    k_lo,
    l_hi,
    l_lo,
    sens_rows,
    sens_slots,
    sens_mat,
    grad_slots,
    load_sem,
    halo_send,
    halo_recv,
    point_send,
    point_recv,
    sens_send,
    sens_recv,
    grad_send,
    grad_recv,
    known,
):
    cells, subs, nodes = (lax.axis_size(a) for a in ("cells", "sub", "nodes"))
    cell_at, sub_at, node_at = (lax.axis_index(a) for a in ("cells", "sub", "nodes"))
    here, places = cell_at * subs + sub_at, cells * subs
    team, crew = node_at * subs + sub_at, nodes * subs
    me, everyone = cell_at * crew + team, cells * crew
    nodes_here = weight_ref.shape[0]
    rows = adj_hbm.shape[1]
    blocks = rows // nodes_here
    cell_count = blocks * LANES
    base_own = base_ref.shape[1]
    panels = base_own // LANES

    def member(index):
        return {"nodes": index // subs, "sub": index % subs}

    def anyone(index):
        return dict(member(index % crew), cells=index // crew)

    lower, upper = cell_at > 0, cell_at < cells - 1
    below, above = cell_at - 1, cell_at + 1
    beside_count = lower.astype(jnp.int32) + upper.astype(jnp.int32)

    base_start = pl.multiple_of(team * base_own, LANES)
    share = pl.ds(base_start, base_own)
    sources = (
        (0, adj_hbm, wide.at[0, :, pl.ds(rows, rows), :]),
        (1, point_hbm, point_ref),
        (2, base_hbm.at[:, share], base_ref),
        (3, nb_hbm, nb_ref),
        (4, off_hbm, off_ref),
        (5, rhs_hbm, rhs_ref),
        (5, inv_hbm, inv_ref),
        (6, sens_hbm, sens_ref),
        (7, ffd_index_hbm.at[:, share], ffd_index_ref),
        (7, ffd_weight_hbm.at[:, share], ffd_weight_ref),
        (8, weight_hbm, weight_ref),
    )
    for group, source, target in sources:
        pltpu.make_async_copy(source, target, load_sem.at[group]).start()

    def arrive(size, sem):
        pltpu.make_async_copy(size, size, sem).wait()

    sizes = [source[2] for source in sources if source[0] not in (5, 7)]
    sizes.insert(5, wide)
    sizes.insert(7, cell_feat.at[0 : 2 * ffd_index_ref.shape[0], 0:base_own])

    def load_wait(*groups):
        for group in groups:
            arrive(sizes[group], load_sem.at[group])

    barrier = pltpu.get_barrier_semaphore()

    def greet(device):
        pl.semaphore_signal(barrier, inc=1, device_id=device, device_id_type=MESH)

    greeted = crew - 1
    for step in range(1, crew):
        greet(member((team + step) % crew))
    greetings = [(lower, {"cells": below}), (upper, {"cells": above})]
    if subs > 1:
        first, last = sub_at == 0, sub_at == subs - 1
        greetings.append((jnp.logical_and(lower, first), {"cells": below, "sub": subs - 1}))
        greetings.append((jnp.logical_and(upper, last), {"cells": above, "sub": 0}))
    for exists, device in greetings:
        pl.when(exists)(functools.partial(greet, device))
        greeted = greeted + exists.astype(jnp.int32)

    def tell(stage):
        for exists, other in ((upper, above), (lower, below)):

            @pl.when(exists)
            def _():
                pl.semaphore_signal(
                    known.at[stage],
                    inc=1,
                    device_id={"cells": other},
                    device_id_type=MESH,
                )

    def hear(stage):
        pl.semaphore_wait(known.at[stage], beside_count)

    @pl.when(here == 0)
    def _():
        wide[:, :, 0:rows, :] = jnp.zeros((SWEEPS, 5, rows, LANES), jnp.float32)

    @pl.when(here == places - 1)
    def _():
        wide[:, :, 2 * rows : 3 * rows, :] = jnp.zeros((SWEEPS, 5, rows, LANES), jnp.float32)

    def halo(sweep, side):
        other = here + 1 if side == 0 else here - 1
        start = 0 if side == 0 else 2 * rows
        return pltpu.make_async_remote_copy(
            src_ref=wide.at[sweep, :, pl.ds(rows, rows), :],
            dst_ref=wide.at[sweep, :, pl.ds(start, rows), :],
            send_sem=halo_send.at[side],
            recv_sem=halo_recv.at[sweep, side],
            device_id={"cells": other // subs, "sub": other % subs},
            device_id_type=MESH,
        )

    def halo_start(sweep):
        @pl.when(here < places - 1)
        def _():
            halo(sweep, 0).start()

        @pl.when(here > 0)
        def _():
            halo(sweep, 1).start()

    def halo_wait(sweep):
        @pl.when(here > 0)
        def _():
            halo(sweep, 0).wait_recv()

        @pl.when(here < places - 1)
        def _():
            halo(sweep, 1).wait_recv()

    def halo_sent():
        both = wide.at[:, :, pl.ds(rows, rows), :]

        @pl.when(here < places - 1)
        def _():
            arrive(both, halo_send.at[0])

        @pl.when(here > 0)
        def _():
            arrive(both, halo_send.at[1])

    def point_copy(step):
        return pltpu.make_async_remote_copy(
            src_ref=point_ref,
            dst_ref=points.at[step],
            send_sem=point_send.at[step],
            recv_sem=point_recv.at[step],
            device_id={"sub": (sub_at + step) % subs},
            device_id_type=MESH,
        )

    load_wait(0, 1)
    pl.semaphore_wait(barrier, greeted)
    halo_start(0)
    for step in range(1, subs):
        point_copy(step).start()
    tell(0)

    load_wait(2, 3)
    first_cell = here * cell_count
    for face in range(nb_ref.shape[0]):
        for block in range(blocks):
            entry = nb_ref[face : face + 1, block * LANES : (block + 1) * LANES]
            local = entry - first_cell + cell_count
            chunk = jnp.where(entry >= 0, (local >> 7) - block, -1)
            span = pl.ds(block * nodes_here, nodes_here)
            rel_ref[face, span, :] = jnp.broadcast_to(chunk, (nodes_here, LANES))
            lane_ref[face, span, :] = jnp.broadcast_to(local & (LANES - 1), (nodes_here, LANES))

    def features(xyz, own):
        one, two, three = split3(xyz)
        square = xyz[0:1] * xyz[0:1] + xyz[1:2] * xyz[1:2] + xyz[2:3] * xyz[2:3]
        pieces = [one, one, two, two, one, three] if own else [one, two, one, two, three, one]
        parts = split3(square)
        ones = jnp.ones_like(square)
        for slot, piece in enumerate(pieces):
            cell_feat[3 * slot : 3 * slot + 3, 0 : xyz.shape[1]] = piece if own else -2.0 * piece
        for slot in range(3):
            cell_feat[18 + slot : 19 + slot, 0 : xyz.shape[1]] = parts[slot] if own else ones
            cell_feat[21 + slot : 22 + slot, 0 : xyz.shape[1]] = ones if own else parts[slot]

    stretch = 4.0 / support_radius
    features((base_ref[...] - 0.5) * stretch, False)
    base_feat[...] = cell_feat[:, 0:base_own].astype(jnp.bfloat16)

    def build_kernel(step):
        xyz = point_ref[...] if step == 0 else points[step]
        features((xyz - 0.5) * stretch, True)
        cell_rows[...] = cell_feat[:, 0:cell_count].T.astype(jnp.bfloat16)
        width = 2 * LANES
        for left in range(0, base_own, width):
            other = base_feat[:, left : left + width]
            for top in range(0, cell_count, PIECE):
                mine = cell_rows[top : top + PIECE, :]
                target = slice(step * cell_count + top, step * cell_count + top + PIECE)
                squared = jnp.dot(mine, other, preferred_element_type=jnp.float32)
                squared = jnp.maximum(squared, 1e-20)
                ratio = squared * lax.rsqrt(squared)
                inside = jnp.maximum(4.0 - ratio, 0.0)
                fourth = inside * inside
                value = (fourth * fourth) * (5.0 - inside)
                for side in range(2):
                    hi, lo = split2(value[:, side * LANES : (side + 1) * LANES])
                    k_hi[left // LANES + side, target, :] = hi
                    k_lo[left // LANES + side, target, :] = lo

    def build_lattice(panel, carry):
        at = pl.ds(pl.multiple_of(panel * LANES, LANES), LANES)
        index, weight = ffd_index_ref[:, at], ffd_weight_ref[:, at]
        slots = index.shape[0]
        slot = lax.broadcasted_iota(jnp.int32, index.shape, 0)
        total, repeat = weight, jnp.zeros(index.shape, jnp.int32)
        for turn in range(1, slots):
            same = pltpu.roll(index, turn, 0) == index
            total = total + jnp.where(same, pltpu.roll(weight, turn, 0), 0.0)
            repeat = jnp.where(jnp.logical_and(same, slot >= turn), 1, repeat)
        index = jnp.where(repeat == 1, -1, index)
        hi = total.astype(jnp.bfloat16).astype(jnp.float32)
        lo = total - hi
        tall = (2 * ROWS, LANES)

        def spread(value, kind):
            return [jnp.broadcast_to(value[s : s + 1], tall).astype(kind) for s in range(slots)]

        index, hi, lo = spread(index, jnp.int16), spread(hi, jnp.bfloat16), spread(lo, jnp.bfloat16)
        row = lax.broadcasted_iota(jnp.int32, tall, 0).astype(jnp.int16)
        for top in range(0, FFD, 2 * ROWS):
            found_hi = found_lo = jnp.zeros(tall, jnp.bfloat16)
            here_row = row + jnp.int16(top)
            for s in range(slots):
                match = index[s] == here_row
                found_hi = jnp.where(match, hi[s], found_hi)
                found_lo = jnp.where(match, lo[s], found_lo)
            l_hi[panel, top : top + 2 * ROWS, :] = found_hi
            l_lo[panel, top : top + 2 * ROWS, :] = found_lo
        return carry

    def relax(sweep):
        pieces, stride = rows // ROWS, ROWS // nodes_here
        zero = jnp.zeros((ROWS, LANES), jnp.float32)
        coupled = [[zero] * 5 for _ in range(pieces)]
        for face in range(off_ref.shape[0]):
            for piece in range(pieces):
                span = slice(piece * ROWS, (piece + 1) * ROWS)
                rel, lane = rel_ref[face, span, :], lane_ref[face, span, :]
                found = [zero] * 5
                for chunk in range(2 * blocks + 1):
                    match = rel == chunk
                    at = (chunk + stride * piece) * nodes_here
                    for comp in range(5):
                        window = wide[sweep, comp, at : at + ROWS, :]
                        taken = jnp.take_along_axis(window, lane, axis=1)
                        found[comp] = jnp.where(match, taken, found[comp])
                for a in range(5):
                    for b in range(5):
                        block = off_ref[face, 5 * a + b, span].astype(jnp.float32)
                        coupled[piece][a] = coupled[piece][a] + block * found[b]
        result = []
        for piece in range(pieces):
            span = slice(piece * ROWS, (piece + 1) * ROWS)
            rest = [rhs_ref[b, span] - coupled[piece][b] for b in range(5)]
            totals = []
            for a in range(5):
                total = inv_ref[5 * a, span] * rest[0]
                for b in range(1, 5):
                    total = total + inv_ref[5 * a + b, span] * rest[b]
                totals.append(total)
            result.append(totals)
        return result

    build_kernel(0)
    load_wait(4, 5)
    halo_wait(0)
    result = relax(0)
    for piece, totals in enumerate(result):
        for a in range(5):
            wide[1, a, rows + piece * ROWS : rows + (piece + 1) * ROWS, :] = totals[a]
    halo_start(1)
    if cells > 2:
        hear(0)
        tell(1)
    for step in range(1, subs):
        point_copy(step).wait_recv()
        build_kernel(step)
    load_wait(6, 7, 8)
    halo_wait(1)
    result = relax(1)
    for piece, totals in enumerate(result):
        span = slice(piece * ROWS, (piece + 1) * ROWS)
        for k in range(3):
            total = totals[0] * sens_ref[k, span].astype(jnp.float32)
            for a in range(1, 5):
                total = total + totals[a] * sens_ref[3 * a + k, span].astype(jnp.float32)
            sens_rows[k, span, :] = total
    for k in range(3):
        total = weight_ref[0] * sens_rows[k, pl.ds(0, blocks, stride=nodes_here), :]
        for n in range(1, nodes_here):
            total = total + weight_ref[n] * sens_rows[k, pl.ds(n, blocks, stride=nodes_here), :]
        sens_slots[team, k] = total

    def sens_copy(step):
        return pltpu.make_async_remote_copy(
            src_ref=sens_slots.at[team],
            dst_ref=sens_slots.at[team],
            send_sem=sens_send,
            recv_sem=sens_recv,
            device_id=member((team + step) % crew),
            device_id_type=MESH,
        )

    for step in range(1, crew):
        sens_copy(step).start()
    for piece, totals in enumerate(result):
        for a in range(5):
            out_ref[a, piece * ROWS : (piece + 1) * ROWS, :] = totals[a]
    for stage in range(2, cells - 1):
        hear(stage - 1)
        tell(stage)
    sens_mat[...] = jnp.zeros_like(sens_mat)
    lax.fori_loop(0, panels, build_lattice, 0)
    arrive(sens_slots.at[pl.ds(0, crew - 1)], sens_recv)
    for step in range(subs):
        whose = (sub_at - step + subs) % subs
        for k in range(3):
            total = sens_slots[whose, k]
            for n in range(1, nodes):
                total = total + sens_slots[n * subs + whose, k]
            hi = total.astype(jnp.bfloat16).astype(jnp.float32)
            lo = total - hi
            for block in range(blocks):
                at = step * cell_count + block * LANES
                sens_mat[k : k + 1, at : at + LANES] = hi[block : block + 1, :]
                sens_mat[ROWS + k : ROWS + k + 1, at : at + LANES] = lo[block : block + 1, :]

    left = sens_mat[...].astype(jnp.bfloat16)
    contract = (((1,), (1,)), ((), ()))
    own = jnp.zeros((2 * ROWS, FFD), jnp.float32)
    grads = []
    for pair in range(0, panels, 2):
        product = jnp.zeros((2 * ROWS, 2 * LANES), jnp.float32)
        for table in (k_hi, k_lo):
            both = jnp.concatenate([table[pair], table[pair + 1]], axis=1)
            product = product + jnp.dot(left, both, preferred_element_type=jnp.float32)
        grads.append((product[0:ROWS] + product[ROWS:]) * scale)
    for pair in range(0, panels, 2):
        base_grad = grads[pair // 2]
        hi = base_grad.astype(jnp.bfloat16).astype(jnp.float32)
        sides = jnp.concatenate([hi, base_grad - hi], axis=0).astype(jnp.bfloat16)
        for table in (l_hi, l_lo):
            both = jnp.concatenate([table[pair], table[pair + 1]], axis=1)
            own = own + lax.dot_general(sides, both, contract, preferred_element_type=jnp.float32)
    own = own[0:ROWS] + own[ROWS:]
    for block in range(FFD // LANES):
        grad_slots[me, 3 * block : 3 * block + 3, :] = own[
            0:3, block * LANES : (block + 1) * LANES
        ]

    def grad_copy(step):
        return pltpu.make_async_remote_copy(
            src_ref=grad_slots.at[me],
            dst_ref=grad_slots.at[me],
            send_sem=grad_send,
            recv_sem=grad_recv,
            device_id=anyone((me + step) % everyone),
            device_id_type=MESH,
        )

    if cells > 1:
        hear(cells - 2)
    for step in range(1, everyone):
        grad_copy(step).start()
    halo_sent()
    for step in range(1, subs):
        point_copy(step).wait_send()
    arrive(sens_slots.at[pl.ds(0, crew - 1)], sens_send)
    others = grad_slots.at[pl.ds(0, everyone - 1)]
    arrive(others, grad_send)
    arrive(others, grad_recv)
    total = grad_slots[0]
    for slot in range(1, everyone):
        total = total + grad_slots[slot]
    for block in range(FFD // LANES):
        grad_ref[:, block * LANES : (block + 1) * LANES] = total[3 * block : 3 * block + 3, :]


def finish(adjoint_in, control_in, adjoint_out, control_out):
    adjoint_out[...] = adjoint_in[...]
    control_out[...] = control_in[...]


def to_rows(array):
    array = jnp.moveaxis(array, 0, -2)
    lead, (nodes, cells) = array.shape[:-2], array.shape[-2:]
    array = array.reshape(lead + (nodes, cells // LANES, LANES))
    array = jnp.swapaxes(array, -3, -2)
    return array.reshape(lead + (nodes * cells // LANES, LANES))


def from_rows(array, nodes):
    lead, rows = array.shape[:-2], array.shape[-2]
    array = array.reshape(lead + (rows // nodes, nodes, LANES))
    array = jnp.swapaxes(array, -3, -2).reshape(lead + (nodes, rows // nodes * LANES))
    return jnp.moveaxis(array, -2, 0)


def body(
    adjoint_start,
    adjoint_rhs,
    off_blocks,
    diag_inverse,
    neighbours,
    node_weights,
    sens_blocks,
    cell_points,
    base_points,
    ffd_index,
    ffd_weight,
):
    nodes_here, _, cell_count = adjoint_start.shape
    faces = off_blocks.shape[1]
    cells, subs, nodes = (lax.axis_size(a) for a in ("cells", "sub", "nodes"))
    crew = nodes * subs
    everyone = cells * crew
    blocks = cell_count // LANES
    rows = blocks * nodes_here
    base_own = base_points.shape[1] // crew
    panels = base_own // LANES
    scale = 1.0 / 256.0 / float(cell_count * cells * subs) ** 0.5
    vmem = pl.BlockSpec(memory_space=pltpu.VMEM)
    hbm = pl.BlockSpec(memory_space=pltpu.HBM)
    f32, bf16 = jnp.float32, jnp.bfloat16
    dma = pltpu.SemaphoreType.DMA
    off_rows, inv_rows = to_rows(off_blocks), to_rows(diag_inverse)
    sens_cells = to_rows(sens_blocks)
    adjoint, control = pl.pallas_call(
        functools.partial(kernel, scale),
        out_shape=(
            jax.ShapeDtypeStruct((5, rows, LANES), f32),
            jax.ShapeDtypeStruct((3, FFD), f32),
        ),
        in_specs=[hbm] * 11,
        out_specs=(vmem, vmem),
        scratch_shapes=[
            pltpu.SMEM(node_weights.shape, f32),
            pltpu.VMEM(cell_points.shape, f32),
            pltpu.VMEM(neighbours.shape, jnp.int32),
            pltpu.VMEM((3, base_own), f32),
            pltpu.VMEM(off_rows.shape, bf16),
            pltpu.VMEM((5, rows, LANES), f32),
            pltpu.VMEM(inv_rows.shape, f32),
            pltpu.VMEM(sens_cells.shape, bf16),
            pltpu.VMEM((ffd_index.shape[1], base_own), jnp.int32),
            pltpu.VMEM((ffd_index.shape[1], base_own), f32),
            pltpu.VMEM((SWEEPS, 5, 3 * rows, LANES), f32),
            pltpu.VMEM((faces, rows, LANES), jnp.int32),
            pltpu.VMEM((faces, rows, LANES), jnp.int32),
            pltpu.VMEM((subs, 3, cell_count), f32),
            pltpu.VMEM((cell_count, 24), bf16),
            pltpu.VMEM((24, max(cell_count, base_own)), f32),
            pltpu.VMEM((24, base_own), bf16),
            pltpu.VMEM((panels, subs * cell_count, LANES), bf16),
            pltpu.VMEM((panels, subs * cell_count, LANES), bf16),
            pltpu.VMEM((panels, FFD, LANES), bf16),
            pltpu.VMEM((panels, FFD, LANES), bf16),
            pltpu.VMEM((3, rows, LANES), f32),
            pltpu.VMEM((crew, 3, blocks, LANES), f32),
            pltpu.VMEM((2 * ROWS, subs * cell_count), f32),
            pltpu.VMEM((everyone, 3 * FFD // LANES, LANES), f32),
            dma((9,)),
            dma((2,)),
            dma((SWEEPS, 2)),
            dma((subs,)),
            dma((subs,)),
            dma,
            dma,
            dma,
            dma,
            pltpu.SemaphoreType.REGULAR((max(cells - 1, 1),)),
        ],
        compiler_params=pltpu.CompilerParams(
            collective_id=0, has_side_effects=True, vmem_limit_bytes=16 * 1024 * 1024
        ),
    )(
        *(pltpu.with_memory_space_constraint(array, pltpu.HBM) for array in (
            node_weights,
            to_rows(adjoint_start),
            cell_points,
            neighbours,
            base_points,
            off_rows,
            to_rows(adjoint_rhs),
            inv_rows,
            sens_cells,
            ffd_index.T,
            ffd_weight.T,
        ))
    )
    adjoint, control = pl.pallas_call(
        finish,
        out_shape=(
            jax.ShapeDtypeStruct((5, rows, LANES), f32),
            jax.ShapeDtypeStruct((3, FFD), f32),
        ),
        in_specs=[vmem] * 2,
        out_specs=(vmem, vmem),
        compiler_params=pltpu.CompilerParams(vmem_limit_bytes=1024 * 1024),
    )(adjoint, control)
    return from_rows(adjoint, nodes_here), control


def solution(mesh):
    return jax.shard_map(
        body,
        mesh=mesh,
        in_specs=(
            P("nodes", None, ("groups", "cells", "sub")),
            P("nodes", None, ("groups", "cells", "sub")),
            P("nodes", None, None, ("groups", "cells", "sub")),
            P("nodes", None, ("groups", "cells", "sub")),
            P(None, ("cells", "sub")),
            P("nodes"),
            P("nodes", None, ("groups", "cells", "sub")),
            P(None, ("cells", "sub")),
            P(),
            P(),
            P(),
        ),
        out_specs=(P("nodes", None, ("groups", "cells", "sub")), P("groups", None)),
        check_vma=False,
    )
```

```python
import functools

import jax
import jax.numpy as jnp
from jax import lax
from jax.experimental import pallas as pl
from jax.experimental.pallas import tpu as pltpu
from jax.sharding import PartitionSpec as P

SWEEPS = 2
FFD = 512
LANES = 128
ROWS = 8
PIECE = 64

support_radius = 0.3
MESH = pl.DeviceIdType.MESH


def split2(x):
    hi = x.astype(jnp.bfloat16)
    return hi, (x - hi.astype(jnp.float32)).astype(jnp.bfloat16)


def split3(x):
    one = x.astype(jnp.bfloat16).astype(jnp.float32)
    two = (x - one).astype(jnp.bfloat16).astype(jnp.float32)
    return one, two, (x - one) - two


def kernel(
    scale,
    weight_hbm,
    adj_hbm,
    point_hbm,
    nb_hbm,
    base_hbm,
    off_hbm,
    rhs_hbm,
    inv_hbm,
    sens_hbm,
    ffd_index_hbm,
    ffd_weight_hbm,
    out_ref,
    grad_ref,
    weight_ref,
    point_ref,
    nb_ref,
    base_ref,
    off_ref,
    rhs_ref,
    inv_ref,
    sens_ref,
    ffd_index_ref,
    ffd_weight_ref,
    wide,
    rel_ref,
    lane_ref,
    found_ref,
    points,
    cell_rows,
    cell_feat,
    base_feat,
    k_hi,
    k_lo,
    l_hi,
    l_lo,
    sens_rows,
    sens_slots,
    sens_mat,
    grad_slots,
    load_sem,
    halo_send,
    halo_recv,
    point_send,
    point_recv,
    sens_send,
    sens_recv,
    grad_send,
    grad_recv,
    known,
):
    cells, subs, nodes = (lax.axis_size(a) for a in ("cells", "sub", "nodes"))
    cell_at, sub_at, node_at = (lax.axis_index(a) for a in ("cells", "sub", "nodes"))
    here, places = cell_at * subs + sub_at, cells * subs
    team, crew = node_at * subs + sub_at, nodes * subs
    me, everyone = cell_at * crew + team, cells * crew
    nodes_here = weight_ref.shape[0]
    rows = adj_hbm.shape[1]
    blocks = rows // nodes_here
    cell_count = blocks * LANES
    base_own = base_ref.shape[1]
    panels = base_own // LANES

    def member(index):
        return {"nodes": index // subs, "sub": index % subs}

    def anyone(index):
        return dict(member(index % crew), cells=index // crew)

    lower, upper = cell_at > 0, cell_at < cells - 1
    below, above = cell_at - 1, cell_at + 1
    beside_count = lower.astype(jnp.int32) + upper.astype(jnp.int32)

    adj_load = pltpu.make_async_copy(
        adj_hbm, wide.at[0, :, pl.ds(rows, rows), :], load_sem.at[0]
    )
    adj_load.start()
    barrier = pltpu.get_barrier_semaphore()

    def greet(device):
        pl.semaphore_signal(barrier, inc=1, device_id=device, device_id_type=MESH)

    greeted = crew - 1
    for step in range(1, crew):
        greet(member((team + step) % crew))
    greetings = [(lower, {"cells": below}), (upper, {"cells": above})]
    if subs > 1:
        first, last = sub_at == 0, sub_at == subs - 1
        greetings.append((jnp.logical_and(lower, first), {"cells": below, "sub": subs - 1}))
        greetings.append((jnp.logical_and(upper, last), {"cells": above, "sub": 0}))
    for exists, device in greetings:
        pl.when(exists)(functools.partial(greet, device))
        greeted = greeted + exists.astype(jnp.int32)

    base_start = pl.multiple_of(team * base_own, LANES)
    share = pl.ds(base_start, base_own)
    sources = (
        (0, adj_hbm, wide.at[0, :, pl.ds(rows, rows), :]),
        (1, point_hbm, point_ref),
        (2, base_hbm.at[:, share], base_ref),
        (3, nb_hbm, nb_ref),
        (4, off_hbm, off_ref),
        (5, rhs_hbm, rhs_ref),
        (5, inv_hbm, inv_ref),
        (6, sens_hbm, sens_ref),
        (7, ffd_index_hbm.at[:, share], ffd_index_ref),
        (7, ffd_weight_hbm.at[:, share], ffd_weight_ref),
        (8, weight_hbm, weight_ref),
    )
    for group, source, target in sources[1:]:
        pltpu.make_async_copy(source, target, load_sem.at[group]).start()

    def arrive(size, sem):
        pltpu.make_async_copy(size, size, sem).wait()

    sizes = [source[2] for source in sources if source[0] not in (5, 7)]
    sizes.insert(5, wide)
    sizes.insert(7, cell_feat.at[0 : 2 * ffd_index_ref.shape[0], 0:base_own])

    def load_wait(*groups):
        for group in groups:
            arrive(sizes[group], load_sem.at[group])

    def tell(stage):
        for exists, other in ((upper, above), (lower, below)):

            @pl.when(exists)
            def _():
                pl.semaphore_signal(
                    known.at[stage],
                    inc=1,
                    device_id={"cells": other},
                    device_id_type=MESH,
                )

    def hear(stage):
        pl.semaphore_wait(known.at[stage], beside_count)

    @pl.when(here == 0)
    def _():
        wide[:, :, 0:rows, :] = jnp.zeros((SWEEPS, 5, rows, LANES), jnp.float32)

    @pl.when(here == places - 1)
    def _():
        wide[:, :, 2 * rows : 3 * rows, :] = jnp.zeros((SWEEPS, 5, rows, LANES), jnp.float32)

    def halo(sweep, side):
        other = here + 1 if side == 0 else here - 1
        start = 0 if side == 0 else 2 * rows
        return pltpu.make_async_remote_copy(
            src_ref=wide.at[sweep, :, pl.ds(rows, rows), :],
            dst_ref=wide.at[sweep, :, pl.ds(start, rows), :],
            send_sem=halo_send.at[side],
            recv_sem=halo_recv.at[sweep, side],
            device_id={"cells": other // subs, "sub": other % subs},
            device_id_type=MESH,
        )

    def halo_start(sweep):
        @pl.when(here < places - 1)
        def _():
            halo(sweep, 0).start()

        @pl.when(here > 0)
        def _():
            halo(sweep, 1).start()

    def halo_sent():
        both = wide.at[:, :, pl.ds(rows, rows), :]

        @pl.when(here < places - 1)
        def _():
            arrive(both, halo_send.at[0])

        @pl.when(here > 0)
        def _():
            arrive(both, halo_send.at[1])

    def point_copy(step):
        return pltpu.make_async_remote_copy(
            src_ref=point_ref,
            dst_ref=points.at[step],
            send_sem=point_send.at[step],
            recv_sem=point_recv.at[step],
            device_id={"sub": (sub_at + step) % subs},
            device_id_type=MESH,
        )

    load_wait(0, 1)
    pl.semaphore_wait(barrier, greeted)
    halo_start(0)
    for step in range(1, subs):
        point_copy(step).start()
    tell(0)

    load_wait(2, 3)
    first_cell = here * cell_count
    for face in range(nb_ref.shape[0]):
        for block in range(blocks):
            entry = nb_ref[face : face + 1, block * LANES : (block + 1) * LANES]
            local = entry - first_cell + cell_count
            chunk = jnp.where(entry >= 0, (local >> 7) - block, -1)
            span = pl.ds(block * nodes_here, nodes_here)
            rel_ref[face, span, :] = jnp.broadcast_to(chunk, (nodes_here, LANES))
            lane_ref[face, span, :] = jnp.broadcast_to(local & (LANES - 1), (nodes_here, LANES))

    def features(xyz, own):
        one, two, three = split3(xyz)
        square = xyz[0:1] * xyz[0:1] + xyz[1:2] * xyz[1:2] + xyz[2:3] * xyz[2:3]
        pieces = [one, one, two, two, one, three] if own else [one, two, one, two, three, one]
        parts = split3(square)
        ones = jnp.ones_like(square)
        for slot, piece in enumerate(pieces):
            cell_feat[3 * slot : 3 * slot + 3, 0 : xyz.shape[1]] = piece if own else -2.0 * piece
        for slot in range(3):
            cell_feat[18 + slot : 19 + slot, 0 : xyz.shape[1]] = parts[slot] if own else ones
            cell_feat[21 + slot : 22 + slot, 0 : xyz.shape[1]] = ones if own else parts[slot]

    stretch = 4.0 / support_radius
    features((base_ref[...] - 0.5) * stretch, False)
    base_feat[...] = cell_feat[:, 0:base_own].astype(jnp.bfloat16)

    def build_features(step):
        xyz = point_ref[...] if step == 0 else points[step]
        features((xyz - 0.5) * stretch, True)
        cell_rows[...] = cell_feat[:, 0:cell_count].T.astype(jnp.bfloat16)

    def build_kernel(step, begin, end):
        width = 2 * LANES
        for left in range(begin, end, width):
            other = base_feat[:, left : left + width]
            for top in range(0, cell_count, PIECE):
                mine = cell_rows[top : top + PIECE, :]
                target = slice(step * cell_count + top, step * cell_count + top + PIECE)
                squared = jnp.dot(mine, other, preferred_element_type=jnp.float32)
                squared = jnp.maximum(squared, 1e-20)
                ratio = squared * lax.rsqrt(squared)
                inside = jnp.maximum(4.0 - ratio, 0.0)
                fourth = inside * inside
                value = (fourth * fourth) * (5.0 - inside)
                for side in range(2):
                    hi, lo = split2(value[:, side * LANES : (side + 1) * LANES])
                    k_hi[left // LANES + side, target, :] = hi
                    k_lo[left // LANES + side, target, :] = lo

    def build_lattice(panel, carry):
        at = pl.ds(pl.multiple_of(panel * LANES, LANES), LANES)
        index, weight = ffd_index_ref[:, at], ffd_weight_ref[:, at]
        slots = index.shape[0]
        slot = lax.broadcasted_iota(jnp.int32, index.shape, 0)
        total, repeat = weight, jnp.zeros(index.shape, jnp.int32)
        for turn in range(1, slots):
            same = pltpu.roll(index, turn, 0) == index
            total = total + jnp.where(same, pltpu.roll(weight, turn, 0), 0.0)
            repeat = jnp.where(jnp.logical_and(same, slot >= turn), 1, repeat)
        index = jnp.where(repeat == 1, -1, index)
        hi = total.astype(jnp.bfloat16).astype(jnp.float32)
        lo = total - hi
        tall = (2 * ROWS, LANES)

        def spread(value, kind):
            return [jnp.broadcast_to(value[s : s + 1], tall).astype(kind) for s in range(slots)]

        index, hi, lo = spread(index, jnp.int16), spread(hi, jnp.bfloat16), spread(lo, jnp.bfloat16)
        row = lax.broadcasted_iota(jnp.int32, tall, 0).astype(jnp.int16)
        for top in range(0, FFD, 2 * ROWS):
            found_hi = found_lo = jnp.zeros(tall, jnp.bfloat16)
            here_row = row + jnp.int16(top)
            for s in range(slots):
                match = index[s] == here_row
                found_hi = jnp.where(match, hi[s], found_hi)
                found_lo = jnp.where(match, lo[s], found_lo)
            l_hi[panel, top : top + 2 * ROWS, :] = found_hi
            l_lo[panel, top : top + 2 * ROWS, :] = found_lo
        return carry

    pieces, stride = rows // ROWS, ROWS // nodes_here
    zero = jnp.zeros((ROWS, LANES), jnp.float32)

    def arrives_late(piece, chunk, far_low, far_high):
        first_row = chunk + stride * piece
        last_row = first_row + stride - 1
        return (far_low and first_row < blocks) or (far_high and last_row >= 2 * blocks)

    def seek(sweep, face, piece, found, chunks):
        span = slice(piece * ROWS, (piece + 1) * ROWS)
        rel, lane = rel_ref[face, span, :], lane_ref[face, span, :]
        for chunk in chunks:
            match = rel == chunk
            at = (chunk + stride * piece) * nodes_here
            for comp in range(5):
                window = wide[sweep, comp, at : at + ROWS, :]
                taken = jnp.take_along_axis(window, lane, axis=1)
                found[comp] = jnp.where(match, taken, found[comp])
        return found

    def chunk_lists(piece, far):
        late = [c for c in range(2 * blocks + 1) if arrives_late(piece, c, *far)]
        return [c for c in range(2 * blocks + 1) if c not in late], late

    def relax_early(sweep, far):
        for face in range(off_ref.shape[0]):
            for piece in range(pieces):
                found = seek(sweep, face, piece, [zero] * 5, chunk_lists(piece, far)[0])
                for comp in range(5):
                    found_ref[face, piece, comp] = found[comp]

    def relax_late(sweep, far):
        for piece in range(pieces):
            span = slice(piece * ROWS, (piece + 1) * ROWS)
            coupled = [zero] * 5
            for face in range(off_ref.shape[0]):
                found = [found_ref[face, piece, comp] for comp in range(5)]
                found = seek(sweep, face, piece, found, chunk_lists(piece, far)[1])
                for a in range(5):
                    for b in range(5):
                        block = off_ref[face, 5 * a + b, span].astype(jnp.float32)
                        coupled[a] = coupled[a] + block * found[b]
            rest = [rhs_ref[b, span] - coupled[b] for b in range(5)]
            for a in range(5):
                total = inv_ref[5 * a, span] * rest[0]
                for b in range(1, 5):
                    total = total + inv_ref[5 * a + b, span] * rest[b]
                if sweep + 1 < SWEEPS:
                    at = rows + piece * ROWS
                    wide[sweep + 1, a, at : at + ROWS, :] = total
                else:
                    out_ref[a, span] = total

    def by_side(work, sweep):
        for far in sorted({(s == 0, s == subs - 1) for s in range(subs)}):
            same = jnp.logical_and(
                (sub_at == 0) == far[0], (sub_at == subs - 1) == far[1]
            )
            pl.when(same)(functools.partial(work, sweep, far))

    def halo_near(sweep):
        @pl.when(sub_at > 0)
        def _():
            halo(sweep, 0).wait_recv()

        @pl.when(sub_at < subs - 1)
        def _():
            halo(sweep, 1).wait_recv()

    def halo_far(sweep):
        @pl.when(jnp.logical_and(sub_at == 0, here > 0))
        def _():
            halo(sweep, 0).wait_recv()

        @pl.when(jnp.logical_and(sub_at == subs - 1, here < places - 1))
        def _():
            halo(sweep, 1).wait_recv()

    split = max(base_own // 2 // (2 * LANES), 1) * 2 * LANES
    halo_near(0)
    by_side(relax_early, 0)
    build_features(0)
    build_kernel(0, 0, base_own)
    load_wait(4, 5)
    halo_far(0)
    by_side(relax_late, 0)
    halo_start(1)
    if cells > 2:
        hear(0)
        tell(1)
    for step in range(1, subs):
        point_copy(step).wait_recv()
        build_features(step)
        build_kernel(step, 0, split if step == subs - 1 else base_own)
    load_wait(6, 7, 8)
    halo_near(1)
    by_side(relax_early, 1)
    halo_far(1)
    by_side(relax_late, 1)
    for k in range(3):
        total = out_ref[0] * sens_ref[k].astype(jnp.float32)
        for a in range(1, 5):
            total = total + out_ref[a] * sens_ref[3 * a + k].astype(jnp.float32)
        sens_rows[k] = total
    for k in range(3):
        total = weight_ref[0] * sens_rows[k, pl.ds(0, blocks, stride=nodes_here), :]
        for n in range(1, nodes_here):
            total = total + weight_ref[n] * sens_rows[k, pl.ds(n, blocks, stride=nodes_here), :]
        sens_slots[team, k] = total

    def sens_copy(step):
        return pltpu.make_async_remote_copy(
            src_ref=sens_slots.at[team],
            dst_ref=sens_slots.at[team],
            send_sem=sens_send,
            recv_sem=sens_recv,
            device_id=member((team + step) % crew),
            device_id_type=MESH,
        )

    for step in range(1, crew):
        sens_copy(step).start()
    for stage in range(2, cells - 1):
        hear(stage - 1)
        tell(stage)
    sens_mat[...] = jnp.zeros_like(sens_mat)
    if subs > 1:
        build_kernel(subs - 1, split, base_own)
    lax.fori_loop(0, panels, build_lattice, 0)
    arrive(sens_slots.at[pl.ds(0, crew - 1)], sens_recv)
    for step in range(subs):
        whose = (sub_at - step + subs) % subs
        for k in range(3):
            total = sens_slots[whose, k]
            for n in range(1, nodes):
                total = total + sens_slots[n * subs + whose, k]
            hi = total.astype(jnp.bfloat16).astype(jnp.float32)
            lo = total - hi
            for block in range(blocks):
                at = step * cell_count + block * LANES
                sens_mat[k : k + 1, at : at + LANES] = hi[block : block + 1, :]
                sens_mat[ROWS + k : ROWS + k + 1, at : at + LANES] = lo[block : block + 1, :]

    left = sens_mat[...].astype(jnp.bfloat16)
    contract = (((1,), (1,)), ((), ()))
    own = jnp.zeros((2 * ROWS, FFD), jnp.float32)
    grads = []
    for pair in range(0, panels, 2):
        product = jnp.zeros((2 * ROWS, 2 * LANES), jnp.float32)
        for table in (k_hi, k_lo):
            both = jnp.concatenate([table[pair], table[pair + 1]], axis=1)
            product = product + jnp.dot(left, both, preferred_element_type=jnp.float32)
        grads.append((product[0:ROWS] + product[ROWS:]) * scale)
    for pair in range(0, panels, 2):
        base_grad = grads[pair // 2]
        hi = base_grad.astype(jnp.bfloat16).astype(jnp.float32)
        sides = jnp.concatenate([hi, base_grad - hi], axis=0).astype(jnp.bfloat16)
        for table in (l_hi, l_lo):
            both = jnp.concatenate([table[pair], table[pair + 1]], axis=1)
            own = own + lax.dot_general(sides, both, contract, preferred_element_type=jnp.float32)
    own = own[0:ROWS] + own[ROWS:]
    for block in range(FFD // LANES):
        grad_slots[me, 3 * block : 3 * block + 3, :] = own[
            0:3, block * LANES : (block + 1) * LANES
        ]

    def grad_copy(step):
        return pltpu.make_async_remote_copy(
            src_ref=grad_slots.at[me],
            dst_ref=grad_slots.at[me],
            send_sem=grad_send,
            recv_sem=grad_recv,
            device_id=anyone((me + step) % everyone),
            device_id_type=MESH,
        )

    if cells > 1:
        hear(cells - 2)
    for step in range(1, everyone):
        grad_copy(step).start()
    halo_sent()
    for step in range(1, subs):
        point_copy(step).wait_send()
    arrive(sens_slots.at[pl.ds(0, crew - 1)], sens_send)
    others = grad_slots.at[pl.ds(0, everyone - 1)]
    arrive(others, grad_send)
    arrive(others, grad_recv)
    total = grad_slots[0]
    for slot in range(1, everyone):
        total = total + grad_slots[slot]
    for block in range(FFD // LANES):
        grad_ref[:, block * LANES : (block + 1) * LANES] = total[3 * block : 3 * block + 3, :]


def finish(adjoint_in, control_in, adjoint_out, control_out):
    adjoint_out[...] = adjoint_in[...]
    control_out[...] = control_in[...]


def to_rows(array):
    array = jnp.moveaxis(array, 0, -2)
    lead, (nodes, cells) = array.shape[:-2], array.shape[-2:]
    array = array.reshape(lead + (nodes, cells // LANES, LANES))
    array = jnp.swapaxes(array, -3, -2)
    return array.reshape(lead + (nodes * cells // LANES, LANES))


def from_rows(array, nodes):
    lead, rows = array.shape[:-2], array.shape[-2]
    array = array.reshape(lead + (rows // nodes, nodes, LANES))
    array = jnp.swapaxes(array, -3, -2).reshape(lead + (nodes, rows // nodes * LANES))
    return jnp.moveaxis(array, -2, 0)


def body(
    adjoint_start,
    adjoint_rhs,
    off_blocks,
    diag_inverse,
    neighbours,
    node_weights,
    sens_blocks,
    cell_points,
    base_points,
    ffd_index,
    ffd_weight,
):
    nodes_here, _, cell_count = adjoint_start.shape
    faces = off_blocks.shape[1]
    cells, subs, nodes = (lax.axis_size(a) for a in ("cells", "sub", "nodes"))
    crew = nodes * subs
    everyone = cells * crew
    blocks = cell_count // LANES
    rows = blocks * nodes_here
    base_own = base_points.shape[1] // crew
    panels = base_own // LANES
    scale = 1.0 / 256.0 / float(cell_count * cells * subs) ** 0.5
    vmem = pl.BlockSpec(memory_space=pltpu.VMEM)
    hbm = pl.BlockSpec(memory_space=pltpu.HBM)
    f32, bf16 = jnp.float32, jnp.bfloat16
    dma = pltpu.SemaphoreType.DMA
    off_rows, inv_rows = to_rows(off_blocks), to_rows(diag_inverse)
    sens_cells = to_rows(sens_blocks)
    adjoint, control = pl.pallas_call(
        functools.partial(kernel, scale),
        out_shape=(
            jax.ShapeDtypeStruct((5, rows, LANES), f32),
            jax.ShapeDtypeStruct((3, FFD), f32),
        ),
        in_specs=[hbm] * 11,
        out_specs=(vmem, vmem),
        scratch_shapes=[
            pltpu.SMEM(node_weights.shape, f32),
            pltpu.VMEM(cell_points.shape, f32),
            pltpu.VMEM(neighbours.shape, jnp.int32),
            pltpu.VMEM((3, base_own), f32),
            pltpu.VMEM(off_rows.shape, bf16),
            pltpu.VMEM((5, rows, LANES), f32),
            pltpu.VMEM(inv_rows.shape, f32),
            pltpu.VMEM(sens_cells.shape, bf16),
            pltpu.VMEM((ffd_index.shape[1], base_own), jnp.int32),
            pltpu.VMEM((ffd_index.shape[1], base_own), f32),
            pltpu.VMEM((SWEEPS, 5, 3 * rows, LANES), f32),
            pltpu.VMEM((faces, rows, LANES), jnp.int32),
            pltpu.VMEM((faces, rows, LANES), jnp.int32),
            pltpu.VMEM((faces, rows // ROWS, 5, ROWS, LANES), f32),
            pltpu.VMEM((subs, 3, cell_count), f32),
            pltpu.VMEM((cell_count, 24), bf16),
            pltpu.VMEM((24, max(cell_count, base_own)), f32),
            pltpu.VMEM((24, base_own), bf16),
            pltpu.VMEM((panels, subs * cell_count, LANES), bf16),
            pltpu.VMEM((panels, subs * cell_count, LANES), bf16),
            pltpu.VMEM((panels, FFD, LANES), bf16),
            pltpu.VMEM((panels, FFD, LANES), bf16),
            pltpu.VMEM((3, rows, LANES), f32),
            pltpu.VMEM((crew, 3, blocks, LANES), f32),
            pltpu.VMEM((2 * ROWS, subs * cell_count), f32),
            pltpu.VMEM((everyone, 3 * FFD // LANES, LANES), f32),
            dma((9,)),
            dma((2,)),
            dma((SWEEPS, 2)),
            dma((subs,)),
            dma((subs,)),
            dma,
            dma,
            dma,
            dma,
            pltpu.SemaphoreType.REGULAR((max(cells - 1, 1),)),
        ],
        compiler_params=pltpu.CompilerParams(
            collective_id=0, has_side_effects=True, vmem_limit_bytes=16 * 1024 * 1024
        ),
    )(
        *(pltpu.with_memory_space_constraint(array, pltpu.HBM) for array in (
            node_weights,
            to_rows(adjoint_start),
            cell_points,
            neighbours,
            base_points,
            off_rows,
            to_rows(adjoint_rhs),
            inv_rows,
            sens_cells,
            ffd_index.T,
            ffd_weight.T,
        ))
    )
    adjoint, control = pl.pallas_call(
        finish,
        out_shape=(
            jax.ShapeDtypeStruct((5, rows, LANES), f32),
            jax.ShapeDtypeStruct((3, FFD), f32),
        ),
        in_specs=[vmem] * 2,
        out_specs=(vmem, vmem),
        compiler_params=pltpu.CompilerParams(vmem_limit_bytes=1024 * 1024),
    )(adjoint, control)
    return from_rows(adjoint, nodes_here), control


def solution(mesh):
    return jax.shard_map(
        body,
        mesh=mesh,
        in_specs=(
            P("nodes", None, ("groups", "cells", "sub")),
            P("nodes", None, ("groups", "cells", "sub")),
            P("nodes", None, None, ("groups", "cells", "sub")),
            P("nodes", None, ("groups", "cells", "sub")),
            P(None, ("cells", "sub")),
            P("nodes"),
            P("nodes", None, ("groups", "cells", "sub")),
            P(None, ("cells", "sub")),
            P(),
            P(),
            P(),
        ),
        out_specs=(P("nodes", None, ("groups", "cells", "sub")), P("groups", None)),
        check_vma=False,
    )
```

```python
import functools

import jax
import jax.numpy as jnp
from jax import lax
from jax.experimental import pallas as pl
from jax.experimental.pallas import tpu as pltpu
from jax.sharding import PartitionSpec as P

SWEEPS = 2
FFD = 512
LANES = 128
ROWS = 8
PIECE = 64

support_radius = 0.3
MESH = pl.DeviceIdType.MESH


def split2(x):
    hi = x.astype(jnp.bfloat16)
    return hi, (x - hi.astype(jnp.float32)).astype(jnp.bfloat16)


def split3(x):
    one = x.astype(jnp.bfloat16).astype(jnp.float32)
    two = (x - one).astype(jnp.bfloat16).astype(jnp.float32)
    return one, two, (x - one) - two


def kernel(
    scale,
    weight_hbm,
    adj_hbm,
    point_hbm,
    nb_hbm,
    base_hbm,
    off_hbm,
    rhs_hbm,
    inv_hbm,
    sens_hbm,
    ffd_index_hbm,
    ffd_weight_hbm,
    out_ref,
    grad_ref,
    weight_ref,
    point_ref,
    nb_ref,
    base_ref,
    off_ref,
    rhs_ref,
    inv_ref,
    sens_ref,
    ffd_index_ref,
    ffd_weight_ref,
    wide,
    rel_ref,
    lane_ref,
    found_ref,
    points,
    cell_rows,
    cell_feat,
    base_feat,
    k_hi,
    k_lo,
    l_hi,
    l_lo,
    sens_rows,
    sens_slots,
    sens_mat,
    grad_slots,
    load_sem,
    halo_send,
    halo_recv,
    point_send,
    point_recv,
    sens_send,
    sens_recv,
    grad_send,
    grad_recv,
    known,
):
    cells, subs, nodes = (lax.axis_size(a) for a in ("cells", "sub", "nodes"))
    cell_at, sub_at, node_at = (lax.axis_index(a) for a in ("cells", "sub", "nodes"))
    here, places = cell_at * subs + sub_at, cells * subs
    team, crew = node_at * subs + sub_at, nodes * subs
    me, everyone = cell_at * crew + team, cells * crew
    nodes_here = weight_ref.shape[0]
    rows = adj_hbm.shape[1]
    blocks = rows // nodes_here
    cell_count = blocks * LANES
    base_own = base_ref.shape[1]
    panels = base_own // LANES

    def member(index):
        return {"nodes": index // subs, "sub": index % subs}

    lower, upper = cell_at > 0, cell_at < cells - 1
    below, above = cell_at - 1, cell_at + 1
    beside_count = lower.astype(jnp.int32) + upper.astype(jnp.int32)

    adj_load = pltpu.make_async_copy(
        adj_hbm, wide.at[0, :, pl.ds(rows, rows), :], load_sem.at[0]
    )
    adj_load.start()
    barrier = pltpu.get_barrier_semaphore()

    def greet(device):
        pl.semaphore_signal(barrier, inc=1, device_id=device, device_id_type=MESH)

    greeted = crew - 1
    for step in range(1, crew):
        greet(member((team + step) % crew))
    greetings = [(lower, {"cells": below}), (upper, {"cells": above})]
    if subs > 1:
        first, last = sub_at == 0, sub_at == subs - 1
        greetings.append((jnp.logical_and(lower, first), {"cells": below, "sub": subs - 1}))
        greetings.append((jnp.logical_and(upper, last), {"cells": above, "sub": 0}))
    for exists, device in greetings:
        pl.when(exists)(functools.partial(greet, device))
        greeted = greeted + exists.astype(jnp.int32)

    base_start = pl.multiple_of(team * base_own, LANES)
    share = pl.ds(base_start, base_own)
    sources = (
        (0, adj_hbm, wide.at[0, :, pl.ds(rows, rows), :]),
        (1, point_hbm, point_ref),
        (2, base_hbm.at[:, share], base_ref),
        (3, nb_hbm, nb_ref),
        (4, off_hbm, off_ref),
        (5, rhs_hbm, rhs_ref),
        (5, inv_hbm, inv_ref),
        (6, sens_hbm, sens_ref),
        (7, ffd_index_hbm.at[:, share], ffd_index_ref),
        (7, ffd_weight_hbm.at[:, share], ffd_weight_ref),
        (8, weight_hbm, weight_ref),
    )
    for group, source, target in sources[1:]:
        pltpu.make_async_copy(source, target, load_sem.at[group]).start()

    def arrive(size, sem):
        pltpu.make_async_copy(size, size, sem).wait()

    sizes = [source[2] for source in sources if source[0] not in (5, 7)]
    sizes.insert(5, wide)
    sizes.insert(7, cell_feat.at[0 : 2 * ffd_index_ref.shape[0], 0:base_own])

    def load_wait(*groups):
        for group in groups:
            arrive(sizes[group], load_sem.at[group])

    def tell(stage):
        for exists, other in ((upper, above), (lower, below)):

            @pl.when(exists)
            def _():
                pl.semaphore_signal(
                    known.at[stage],
                    inc=1,
                    device_id={"cells": other},
                    device_id_type=MESH,
                )

    def hear(stage):
        pl.semaphore_wait(known.at[stage], beside_count)

    @pl.when(here == 0)
    def _():
        wide[:, :, 0:rows, :] = jnp.zeros((SWEEPS, 5, rows, LANES), jnp.float32)

    @pl.when(here == places - 1)
    def _():
        wide[:, :, 2 * rows : 3 * rows, :] = jnp.zeros((SWEEPS, 5, rows, LANES), jnp.float32)

    def halo(sweep, side):
        other = here + 1 if side == 0 else here - 1
        start = 0 if side == 0 else 2 * rows
        return pltpu.make_async_remote_copy(
            src_ref=wide.at[sweep, :, pl.ds(rows, rows), :],
            dst_ref=wide.at[sweep, :, pl.ds(start, rows), :],
            send_sem=halo_send.at[side],
            recv_sem=halo_recv.at[sweep, side],
            device_id={"cells": other // subs, "sub": other % subs},
            device_id_type=MESH,
        )

    def halo_start(sweep):
        @pl.when(here < places - 1)
        def _():
            halo(sweep, 0).start()

        @pl.when(here > 0)
        def _():
            halo(sweep, 1).start()

    def halo_sent():
        both = wide.at[:, :, pl.ds(rows, rows), :]

        @pl.when(here < places - 1)
        def _():
            arrive(both, halo_send.at[0])

        @pl.when(here > 0)
        def _():
            arrive(both, halo_send.at[1])

    def point_copy(step):
        return pltpu.make_async_remote_copy(
            src_ref=point_ref,
            dst_ref=points.at[step],
            send_sem=point_send.at[step - 1],
            recv_sem=point_recv.at[step - 1],
            device_id={"sub": (sub_at + step) % subs},
            device_id_type=MESH,
        )

    load_wait(0, 1)
    pl.semaphore_wait(barrier, greeted)
    halo_start(0)
    for step in range(1, subs):
        point_copy(step).start()
    tell(0)

    load_wait(2, 3)
    first_cell = here * cell_count
    for face in range(nb_ref.shape[0]):
        for block in range(blocks):
            entry = nb_ref[face : face + 1, block * LANES : (block + 1) * LANES]
            local = entry - first_cell + cell_count
            chunk = jnp.where(entry >= 0, (local >> 7) - block, -1)
            span = pl.ds(block * nodes_here, nodes_here)
            rel_ref[face, span, :] = jnp.broadcast_to(chunk, (nodes_here, LANES))
            lane_ref[face, span, :] = jnp.broadcast_to(local & (LANES - 1), (nodes_here, LANES))

    def features(xyz, own):
        one, two, three = split3(xyz)
        square = xyz[0:1] * xyz[0:1] + xyz[1:2] * xyz[1:2] + xyz[2:3] * xyz[2:3]
        pieces = [one, one, two, two, one, three] if own else [one, two, one, two, three, one]
        parts = split3(square)
        ones = jnp.ones_like(square)
        for slot, piece in enumerate(pieces):
            cell_feat[3 * slot : 3 * slot + 3, 0 : xyz.shape[1]] = piece if own else -2.0 * piece
        for slot in range(3):
            cell_feat[18 + slot : 19 + slot, 0 : xyz.shape[1]] = parts[slot] if own else ones
            cell_feat[21 + slot : 22 + slot, 0 : xyz.shape[1]] = ones if own else parts[slot]

    stretch = 4.0 / support_radius
    features((base_ref[...] - 0.5) * stretch, False)
    base_feat[...] = cell_feat[:, 0:base_own].astype(jnp.bfloat16)

    def build_features(step):
        xyz = point_ref[...] if step == 0 else points[step]
        features((xyz - 0.5) * stretch, True)
        cell_rows[...] = cell_feat[:, 0:cell_count].T.astype(jnp.bfloat16)

    width = 2 * LANES

    def build_kernel(step, begin, end):
        for left in range(begin, end, width):
            other = base_feat[:, left : left + width]
            for top in range(0, cell_count, PIECE):
                mine = cell_rows[top : top + PIECE, :]
                target = slice(step * cell_count + top, step * cell_count + top + PIECE)
                squared = jnp.dot(mine, other, preferred_element_type=jnp.float32)
                squared = jnp.maximum(squared, 1e-20)
                ratio = squared * lax.rsqrt(squared)
                inside = jnp.maximum(4.0 - ratio, 0.0)
                fourth = inside * inside
                value = (fourth * fourth) * (5.0 - inside)
                for side in range(2):
                    hi, lo = split2(value[:, side * LANES : (side + 1) * LANES])
                    k_hi[left // LANES + side, target, :] = hi
                    k_lo[left // LANES + side, target, :] = lo

    def build_lattice(panel, carry):
        at = pl.ds(pl.multiple_of(panel * LANES, LANES), LANES)
        index, weight = ffd_index_ref[:, at], ffd_weight_ref[:, at]
        slots = index.shape[0]
        slot = lax.broadcasted_iota(jnp.int32, index.shape, 0)
        total, repeat = weight, jnp.zeros(index.shape, jnp.int32)
        for turn in range(1, slots):
            same = pltpu.roll(index, turn, 0) == index
            total = total + jnp.where(same, pltpu.roll(weight, turn, 0), 0.0)
            repeat = jnp.where(jnp.logical_and(same, slot >= turn), 1, repeat)
        index = jnp.where(repeat == 1, -1, index)
        hi = total.astype(jnp.bfloat16).astype(jnp.float32)
        lo = total - hi
        tall = (2 * ROWS, LANES)

        def spread(value, kind):
            return [jnp.broadcast_to(value[s : s + 1], tall).astype(kind) for s in range(slots)]

        index, hi, lo = spread(index, jnp.int16), spread(hi, jnp.bfloat16), spread(lo, jnp.bfloat16)
        row = lax.broadcasted_iota(jnp.int32, tall, 0).astype(jnp.int16)
        for top in range(0, FFD, 2 * ROWS):
            found_hi = found_lo = jnp.zeros(tall, jnp.bfloat16)
            here_row = row + jnp.int16(top)
            for s in range(slots):
                match = index[s] == here_row
                found_hi = jnp.where(match, hi[s], found_hi)
                found_lo = jnp.where(match, lo[s], found_lo)
            l_hi[panel, top : top + 2 * ROWS, :] = found_hi
            l_lo[panel, top : top + 2 * ROWS, :] = found_lo
        return carry

    pieces, stride = rows // ROWS, ROWS // nodes_here
    zero = jnp.zeros((ROWS, LANES), jnp.float32)

    def arrives_late(piece, chunk, far_low, far_high):
        first_row = chunk + stride * piece
        last_row = first_row + stride - 1
        return (far_low and first_row < blocks) or (far_high and last_row >= 2 * blocks)

    def seek(sweep, face, piece, found, chunks):
        span = slice(piece * ROWS, (piece + 1) * ROWS)
        rel, lane = rel_ref[face, span, :], lane_ref[face, span, :]
        for chunk in chunks:
            match = rel == chunk
            at = (chunk + stride * piece) * nodes_here
            for comp in range(5):
                window = wide[sweep, comp, at : at + ROWS, :]
                taken = jnp.take_along_axis(window, lane, axis=1)
                found[comp] = jnp.where(match, taken, found[comp])
        return found

    def chunk_lists(piece, far):
        late = [c for c in range(2 * blocks + 1) if arrives_late(piece, c, *far)]
        return [c for c in range(2 * blocks + 1) if c not in late], late

    def relax_early(sweep, far):
        for face in range(off_ref.shape[0]):
            for piece in range(pieces):
                found = seek(sweep, face, piece, [zero] * 5, chunk_lists(piece, far)[0])
                for comp in range(5):
                    found_ref[face, piece, comp] = found[comp]

    def relax_late(sweep, far):
        for piece in range(pieces):
            span = slice(piece * ROWS, (piece + 1) * ROWS)
            coupled = [zero] * 5
            for face in range(off_ref.shape[0]):
                found = [found_ref[face, piece, comp] for comp in range(5)]
                found = seek(sweep, face, piece, found, chunk_lists(piece, far)[1])
                for a in range(5):
                    for b in range(5):
                        block = off_ref[face, 5 * a + b, span].astype(jnp.float32)
                        coupled[a] = coupled[a] + block * found[b]
            rest = [rhs_ref[b, span] - coupled[b] for b in range(5)]
            for a in range(5):
                total = inv_ref[5 * a, span] * rest[0]
                for b in range(1, 5):
                    total = total + inv_ref[5 * a + b, span] * rest[b]
                if sweep + 1 < SWEEPS:
                    at = rows + piece * ROWS
                    wide[sweep + 1, a, at : at + ROWS, :] = total
                else:
                    out_ref[a, span] = total

    def by_side(work, sweep):
        for far in sorted({(s == 0, s == subs - 1) for s in range(subs)}):
            same = jnp.logical_and(
                (sub_at == 0) == far[0], (sub_at == subs - 1) == far[1]
            )
            pl.when(same)(functools.partial(work, sweep, far))

    def halo_near(sweep):
        @pl.when(sub_at > 0)
        def _():
            halo(sweep, 0).wait_recv()

        @pl.when(sub_at < subs - 1)
        def _():
            halo(sweep, 1).wait_recv()

    def halo_far(sweep):
        @pl.when(jnp.logical_and(sub_at == 0, here > 0))
        def _():
            halo(sweep, 0).wait_recv()

        @pl.when(jnp.logical_and(sub_at == subs - 1, here < places - 1))
        def _():
            halo(sweep, 1).wait_recv()

    panel_pairs = base_own // width
    first_cut, second_cut = ((panel_pairs * part // 4) * width for part in (1, 2))

    def early_with(step, begin, end):
        def work(sweep, far):
            build_kernel(step, begin, end)
            relax_early(sweep, far)

        return work

    build_features(0)
    build_kernel(0, 0, second_cut)
    halo_near(0)
    by_side(early_with(0, second_cut, base_own), 0)
    load_wait(4, 5)
    halo_far(0)
    by_side(relax_late, 0)
    halo_start(1)
    if cells > 2:
        hear(0)
        tell(1)
    for step in range(1, subs):
        point_copy(step).wait_recv()
        build_features(step)
        build_kernel(step, 0, first_cut if step == subs - 1 else base_own)
    load_wait(6, 7, 8)
    halo_near(1)
    by_side(early_with(subs - 1, first_cut, second_cut if subs > 1 else first_cut), 1)
    halo_far(1)
    by_side(relax_late, 1)
    for k in range(3):
        total = out_ref[0] * sens_ref[k].astype(jnp.float32)
        for a in range(1, 5):
            total = total + out_ref[a] * sens_ref[3 * a + k].astype(jnp.float32)
        sens_rows[k] = total
    for k in range(3):
        total = weight_ref[0] * sens_rows[k, pl.ds(0, blocks, stride=nodes_here), :]
        for n in range(1, nodes_here):
            total = total + weight_ref[n] * sens_rows[k, pl.ds(n, blocks, stride=nodes_here), :]
        sens_slots[team, k] = total

    def sens_copy(node_step, sub_step):
        return pltpu.make_async_remote_copy(
            src_ref=sens_slots.at[team],
            dst_ref=sens_slots.at[team],
            send_sem=sens_send,
            recv_sem=sens_recv,
            device_id={
                "nodes": (node_at + node_step) % nodes,
                "sub": (sub_at + sub_step) % subs,
            },
            device_id_type=MESH,
        )

    crew_steps = [(n, s) for n in range(1, nodes) for s in range(subs)]
    crew_steps += [(0, s) for s in range(1, subs)]
    for node_step, sub_step in crew_steps:
        sens_copy(node_step, sub_step).start()
    for stage in range(2, cells - 1):
        hear(stage - 1)
        tell(stage)
    sens_mat[...] = jnp.zeros_like(sens_mat)
    if subs > 1:
        build_kernel(subs - 1, second_cut, base_own)
    lax.fori_loop(0, panels, build_lattice, 0)
    arrive(sens_slots.at[pl.ds(0, crew - 1)], sens_recv)
    for step in range(subs):
        whose = (sub_at - step + subs) % subs
        for k in range(3):
            total = sens_slots[whose, k]
            for n in range(1, nodes):
                total = total + sens_slots[n * subs + whose, k]
            hi = total.astype(jnp.bfloat16).astype(jnp.float32)
            lo = total - hi
            for block in range(blocks):
                at = step * cell_count + block * LANES
                sens_mat[k : k + 1, at : at + LANES] = hi[block : block + 1, :]
                sens_mat[ROWS + k : ROWS + k + 1, at : at + LANES] = lo[block : block + 1, :]

    left = sens_mat[...].astype(jnp.bfloat16)
    contract = (((1,), (1,)), ((), ()))
    own = jnp.zeros((2 * ROWS, FFD), jnp.float32)
    grads = []
    for pair in range(0, panels, 2):
        product = jnp.zeros((2 * ROWS, 2 * LANES), jnp.float32)
        for table in (k_hi, k_lo):
            both = jnp.concatenate([table[pair], table[pair + 1]], axis=1)
            product = product + jnp.dot(left, both, preferred_element_type=jnp.float32)
        grads.append((product[0:ROWS] + product[ROWS:]) * scale)
    for pair in range(0, panels, 2):
        base_grad = grads[pair // 2]
        hi = base_grad.astype(jnp.bfloat16).astype(jnp.float32)
        sides = jnp.concatenate([hi, base_grad - hi], axis=0).astype(jnp.bfloat16)
        for table in (l_hi, l_lo):
            both = jnp.concatenate([table[pair], table[pair + 1]], axis=1)
            own = own + lax.dot_general(sides, both, contract, preferred_element_type=jnp.float32)
    own = own[0:ROWS] + own[ROWS:]
    for block in range(FFD // LANES):
        grad_slots[me, 3 * block : 3 * block + 3, :] = own[
            0:3, block * LANES : (block + 1) * LANES
        ]

    def grad_copy(cell_step, node_step, sub_step):
        return pltpu.make_async_remote_copy(
            src_ref=grad_slots.at[me],
            dst_ref=grad_slots.at[me],
            send_sem=grad_send,
            recv_sem=grad_recv,
            device_id={
                "cells": (cell_at + cell_step) % cells,
                "nodes": (node_at + node_step) % nodes,
                "sub": (sub_at + sub_step) % subs,
            },
            device_id_type=MESH,
        )

    if cells > 1:
        hear(cells - 2)
    all_steps = [(c,) + step for c in range(1, cells) for step in [(0, 0)] + crew_steps]
    all_steps += [(0,) + step for step in crew_steps]
    for steps in all_steps:
        grad_copy(*steps).start()
    halo_sent()
    for step in range(1, subs):
        point_copy(step).wait_send()
    arrive(sens_slots.at[pl.ds(0, crew - 1)], sens_send)
    others = grad_slots.at[pl.ds(0, everyone - 1)]
    arrive(others, grad_send)
    arrive(others, grad_recv)
    total = grad_slots[0]
    for slot in range(1, everyone):
        total = total + grad_slots[slot]
    for block in range(FFD // LANES):
        grad_ref[:, block * LANES : (block + 1) * LANES] = total[3 * block : 3 * block + 3, :]


def finish(adjoint_in, control_in, adjoint_out, control_out):
    adjoint_out[...] = adjoint_in[...]
    control_out[...] = control_in[...]


def to_rows(array):
    array = jnp.moveaxis(array, 0, -2)
    lead, (nodes, cells) = array.shape[:-2], array.shape[-2:]
    array = array.reshape(lead + (nodes, cells // LANES, LANES))
    array = jnp.swapaxes(array, -3, -2)
    return array.reshape(lead + (nodes * cells // LANES, LANES))


def from_rows(array, nodes):
    lead, rows = array.shape[:-2], array.shape[-2]
    array = array.reshape(lead + (rows // nodes, nodes, LANES))
    array = jnp.swapaxes(array, -3, -2).reshape(lead + (nodes, rows // nodes * LANES))
    return jnp.moveaxis(array, -2, 0)


def body(
    adjoint_start,
    adjoint_rhs,
    off_blocks,
    diag_inverse,
    neighbours,
    node_weights,
    sens_blocks,
    cell_points,
    base_points,
    ffd_index,
    ffd_weight,
):
    nodes_here, _, cell_count = adjoint_start.shape
    faces = off_blocks.shape[1]
    cells, subs, nodes = (lax.axis_size(a) for a in ("cells", "sub", "nodes"))
    crew = nodes * subs
    everyone = cells * crew
    blocks = cell_count // LANES
    rows = blocks * nodes_here
    base_own = base_points.shape[1] // crew
    panels = base_own // LANES
    scale = 1.0 / 256.0 / float(cell_count * cells * subs) ** 0.5
    vmem = pl.BlockSpec(memory_space=pltpu.VMEM)
    hbm = pl.BlockSpec(memory_space=pltpu.HBM)
    f32, bf16 = jnp.float32, jnp.bfloat16
    dma = pltpu.SemaphoreType.DMA
    off_rows, inv_rows = to_rows(off_blocks), to_rows(diag_inverse)
    sens_cells = to_rows(sens_blocks)
    adjoint, control = pl.pallas_call(
        functools.partial(kernel, scale),
        out_shape=(
            jax.ShapeDtypeStruct((5, rows, LANES), f32),
            jax.ShapeDtypeStruct((3, FFD), f32),
        ),
        in_specs=[hbm] * 11,
        out_specs=(vmem, vmem),
        scratch_shapes=[
            pltpu.SMEM(node_weights.shape, f32),
            pltpu.VMEM(cell_points.shape, f32),
            pltpu.VMEM(neighbours.shape, jnp.int32),
            pltpu.VMEM((3, base_own), f32),
            pltpu.VMEM(off_rows.shape, bf16),
            pltpu.VMEM((5, rows, LANES), f32),
            pltpu.VMEM(inv_rows.shape, f32),
            pltpu.VMEM(sens_cells.shape, bf16),
            pltpu.VMEM((ffd_index.shape[1], base_own), jnp.int32),
            pltpu.VMEM((ffd_index.shape[1], base_own), f32),
            pltpu.VMEM((SWEEPS, 5, 3 * rows, LANES), f32),
            pltpu.VMEM((faces, rows, LANES), jnp.int32),
            pltpu.VMEM((faces, rows, LANES), jnp.int32),
            pltpu.VMEM((faces, rows // ROWS, 5, ROWS, LANES), f32),
            pltpu.VMEM((subs, 3, cell_count), f32),
            pltpu.VMEM((cell_count, 24), bf16),
            pltpu.VMEM((24, max(cell_count, base_own)), f32),
            pltpu.VMEM((24, base_own), bf16),
            pltpu.VMEM((panels, subs * cell_count, LANES), bf16),
            pltpu.VMEM((panels, subs * cell_count, LANES), bf16),
            pltpu.VMEM((panels, FFD, LANES), bf16),
            pltpu.VMEM((panels, FFD, LANES), bf16),
            pltpu.VMEM((3, rows, LANES), f32),
            pltpu.VMEM((crew, 3, blocks, LANES), f32),
            pltpu.VMEM((2 * ROWS, subs * cell_count), f32),
            pltpu.VMEM((everyone, 3 * FFD // LANES, LANES), f32),
            dma((9,)),
            dma((2,)),
            dma((SWEEPS, 2)),
            dma((max(subs - 1, 1),)),
            dma((max(subs - 1, 1),)),
            dma,
            dma,
            dma,
            dma,
            pltpu.SemaphoreType.REGULAR((max(cells - 1, 1),)),
        ],
        compiler_params=pltpu.CompilerParams(
            collective_id=0, has_side_effects=True, vmem_limit_bytes=16 * 1024 * 1024
        ),
    )(
        *(pltpu.with_memory_space_constraint(array, pltpu.HBM) for array in (
            node_weights,
            to_rows(adjoint_start),
            cell_points,
            neighbours,
            base_points,
            off_rows,
            to_rows(adjoint_rhs),
            inv_rows,
            sens_cells,
            ffd_index.T,
            ffd_weight.T,
        ))
    )
    adjoint, control = pl.pallas_call(
        finish,
        out_shape=(
            jax.ShapeDtypeStruct((5, rows, LANES), f32),
            jax.ShapeDtypeStruct((3, FFD), f32),
        ),
        in_specs=[vmem] * 2,
        out_specs=(vmem, vmem),
        compiler_params=pltpu.CompilerParams(vmem_limit_bytes=1024 * 1024),
    )(adjoint, control)
    return from_rows(adjoint, nodes_here), control


def solution(mesh):
    return jax.shard_map(
        body,
        mesh=mesh,
        in_specs=(
            P("nodes", None, ("groups", "cells", "sub")),
            P("nodes", None, ("groups", "cells", "sub")),
            P("nodes", None, None, ("groups", "cells", "sub")),
            P("nodes", None, ("groups", "cells", "sub")),
            P(None, ("cells", "sub")),
            P("nodes"),
            P("nodes", None, ("groups", "cells", "sub")),
            P(None, ("cells", "sub")),
            P(),
            P(),
            P(),
        ),
        out_specs=(P("nodes", None, ("groups", "cells", "sub")), P("groups", None)),
        check_vma=False,
    )
```

```python
import functools

import jax
import jax.numpy as jnp
from jax import lax
from jax.experimental import pallas as pl
from jax.experimental.pallas import tpu as pltpu
from jax.sharding import PartitionSpec as P

SWEEPS = 2
FFD = 512
LANES = 128
ROWS = 8
PIECE = 64

support_radius = 0.3
MESH = pl.DeviceIdType.MESH


def split2(x):
    hi = x.astype(jnp.bfloat16)
    return hi, (x - hi.astype(jnp.float32)).astype(jnp.bfloat16)


def split3(x):
    one = x.astype(jnp.bfloat16).astype(jnp.float32)
    two = (x - one).astype(jnp.bfloat16).astype(jnp.float32)
    return one, two, (x - one) - two


def kernel(
    scale,
    weight_hbm,
    adj_hbm,
    point_hbm,
    nb_hbm,
    base_hbm,
    off_hbm,
    rhs_hbm,
    inv_hbm,
    sens_hbm,
    ffd_index_hbm,
    ffd_weight_hbm,
    out_ref,
    grad_ref,
    weight_ref,
    point_ref,
    nb_ref,
    base_ref,
    off_ref,
    rhs_ref,
    inv_ref,
    sens_ref,
    ffd_index_ref,
    ffd_weight_ref,
    wide,
    rel_ref,
    lane_ref,
    found_ref,
    points,
    cell_rows,
    cell_feat,
    base_feat,
    k_hi,
    k_lo,
    l_hi,
    l_lo,
    sens_rows,
    sens_slots,
    sens_mat,
    grad_slots,
    load_sem,
    halo_send,
    halo_recv,
    point_send,
    point_recv,
    sens_send,
    sens_recv,
    grad_send,
    grad_recv,
    known,
    met,
):
    cells, subs, nodes = (lax.axis_size(a) for a in ("cells", "sub", "nodes"))
    cell_at, sub_at, node_at = (lax.axis_index(a) for a in ("cells", "sub", "nodes"))
    here, places = cell_at * subs + sub_at, cells * subs
    team, crew = node_at * subs + sub_at, nodes * subs
    me, everyone = cell_at * crew + team, cells * crew
    nodes_here = weight_ref.shape[0]
    rows = adj_hbm.shape[1]
    blocks = rows // nodes_here
    cell_count = blocks * LANES
    base_own = base_ref.shape[1]
    panels = base_own // LANES

    lower, upper = cell_at > 0, cell_at < cells - 1
    below, above = cell_at - 1, cell_at + 1
    beside_count = lower.astype(jnp.int32) + upper.astype(jnp.int32)

    adj_load = pltpu.make_async_copy(
        adj_hbm, wide.at[0, :, pl.ds(rows, rows), :], load_sem.at[0]
    )
    adj_load.start()
    barrier = pltpu.get_barrier_semaphore()

    def greet(device):
        pl.semaphore_signal(barrier, inc=1, device_id=device, device_id_type=MESH)

    contact = sub_at == subs - 1
    greeted = subs - 1 + contact.astype(jnp.int32) * (nodes - 1)
    for step in range(1, nodes):
        pl.when(contact)(functools.partial(greet, {"nodes": (node_at + step) % nodes}))
    for step in range(1, subs):
        greet({"sub": (sub_at + step) % subs})
    greetings = [(lower, {"cells": below}), (upper, {"cells": above})]
    if subs > 1:
        first, last = sub_at == 0, sub_at == subs - 1
        greetings.append((jnp.logical_and(lower, first), {"cells": below, "sub": subs - 1}))
        greetings.append((jnp.logical_and(upper, last), {"cells": above, "sub": 0}))
    for exists, device in greetings:
        pl.when(exists)(functools.partial(greet, device))
        greeted = greeted + exists.astype(jnp.int32)

    base_start = pl.multiple_of(team * base_own, LANES)
    share = pl.ds(base_start, base_own)
    sources = (
        (0, adj_hbm, wide.at[0, :, pl.ds(rows, rows), :]),
        (1, point_hbm, point_ref),
        (2, base_hbm.at[:, share], base_ref),
        (3, nb_hbm, nb_ref),
        (4, off_hbm, off_ref),
        (5, rhs_hbm, rhs_ref),
        (5, inv_hbm, inv_ref),
        (6, sens_hbm, sens_ref),
        (7, ffd_index_hbm.at[:, share], ffd_index_ref),
        (7, ffd_weight_hbm.at[:, share], ffd_weight_ref),
        (8, weight_hbm, weight_ref),
    )
    for group, source, target in sources[1:]:
        pltpu.make_async_copy(source, target, load_sem.at[group]).start()

    def arrive(size, sem):
        pltpu.make_async_copy(size, size, sem).wait()

    sizes = [source[2] for source in sources if source[0] not in (5, 7)]
    sizes.insert(5, wide)
    sizes.insert(7, cell_feat.at[0 : 2 * ffd_index_ref.shape[0], 0:base_own])

    def load_wait(*groups):
        for group in groups:
            arrive(sizes[group], load_sem.at[group])

    def tell(stage):
        for exists, other in ((upper, above), (lower, below)):

            @pl.when(exists)
            def _():
                pl.semaphore_signal(
                    known.at[stage],
                    inc=1,
                    device_id={"cells": other},
                    device_id_type=MESH,
                )

    def hear(stage):
        pl.semaphore_wait(known.at[stage], beside_count)

    def announce():
        @pl.when(contact)
        def _():
            for step in range(1, nodes):
                pl.semaphore_signal(
                    met.at[0],
                    inc=1,
                    device_id={"nodes": (node_at + step) % nodes},
                    device_id_type=MESH,
                )

    def pass_on():
        @pl.when(contact)
        def _():
            if nodes > 1:
                pl.semaphore_wait(met.at[0], nodes - 1)
            for step in range(1, subs):
                pl.semaphore_signal(
                    met.at[1],
                    inc=1,
                    device_id={"sub": (sub_at + step) % subs},
                    device_id_type=MESH,
                )

    def crew_known():
        @pl.when(jnp.logical_not(contact))
        def _():
            pl.semaphore_wait(met.at[1], 1)

    @pl.when(here == 0)
    def _():
        wide[:, :, 0:rows, :] = jnp.zeros((SWEEPS, 5, rows, LANES), jnp.float32)

    @pl.when(here == places - 1)
    def _():
        wide[:, :, 2 * rows : 3 * rows, :] = jnp.zeros((SWEEPS, 5, rows, LANES), jnp.float32)

    def halo(sweep, side):
        other = here + 1 if side == 0 else here - 1
        start = 0 if side == 0 else 2 * rows
        return pltpu.make_async_remote_copy(
            src_ref=wide.at[sweep, :, pl.ds(rows, rows), :],
            dst_ref=wide.at[sweep, :, pl.ds(start, rows), :],
            send_sem=halo_send.at[side],
            recv_sem=halo_recv.at[sweep, side],
            device_id={"cells": other // subs, "sub": other % subs},
            device_id_type=MESH,
        )

    def halo_start(sweep):
        @pl.when(here < places - 1)
        def _():
            halo(sweep, 0).start()

        @pl.when(here > 0)
        def _():
            halo(sweep, 1).start()

    def halo_sent():
        both = wide.at[:, :, pl.ds(rows, rows), :]

        @pl.when(here < places - 1)
        def _():
            arrive(both, halo_send.at[0])

        @pl.when(here > 0)
        def _():
            arrive(both, halo_send.at[1])

    def point_copy(step):
        return pltpu.make_async_remote_copy(
            src_ref=point_ref,
            dst_ref=points.at[step],
            send_sem=point_send.at[step - 1],
            recv_sem=point_recv.at[step - 1],
            device_id={"sub": (sub_at + step) % subs},
            device_id_type=MESH,
        )

    load_wait(0, 1)
    pl.semaphore_wait(barrier, greeted)
    halo_start(0)
    for step in range(1, subs):
        point_copy(step).start()
    announce()

    load_wait(2, 3)
    first_cell = here * cell_count
    for face in range(nb_ref.shape[0]):
        for block in range(blocks):
            entry = nb_ref[face : face + 1, block * LANES : (block + 1) * LANES]
            local = entry - first_cell + cell_count
            chunk = jnp.where(entry >= 0, (local >> 7) - block, -1)
            span = pl.ds(block * nodes_here, nodes_here)
            rel_ref[face, span, :] = jnp.broadcast_to(chunk, (nodes_here, LANES))
            lane_ref[face, span, :] = jnp.broadcast_to(local & (LANES - 1), (nodes_here, LANES))

    def features(xyz, own):
        one, two, three = split3(xyz)
        square = xyz[0:1] * xyz[0:1] + xyz[1:2] * xyz[1:2] + xyz[2:3] * xyz[2:3]
        pieces = [one, one, two, two, one, three] if own else [one, two, one, two, three, one]
        parts = split3(square)
        ones = jnp.ones_like(square)
        for slot, piece in enumerate(pieces):
            cell_feat[3 * slot : 3 * slot + 3, 0 : xyz.shape[1]] = piece if own else -2.0 * piece
        for slot in range(3):
            cell_feat[18 + slot : 19 + slot, 0 : xyz.shape[1]] = parts[slot] if own else ones
            cell_feat[21 + slot : 22 + slot, 0 : xyz.shape[1]] = ones if own else parts[slot]

    stretch = 4.0 / support_radius
    features((base_ref[...] - 0.5) * stretch, False)
    base_feat[...] = cell_feat[:, 0:base_own].astype(jnp.bfloat16)

    def build_features(step):
        xyz = point_ref[...] if step == 0 else points[step]
        features((xyz - 0.5) * stretch, True)
        cell_rows[...] = cell_feat[:, 0:cell_count].T.astype(jnp.bfloat16)

    width = 2 * LANES

    def build_kernel(step, begin, end):
        for left in range(begin, end, width):
            other = base_feat[:, left : left + width]
            for top in range(0, cell_count, PIECE):
                mine = cell_rows[top : top + PIECE, :]
                target = slice(step * cell_count + top, step * cell_count + top + PIECE)
                squared = jnp.dot(mine, other, preferred_element_type=jnp.float32)
                squared = jnp.maximum(squared, 1e-20)
                ratio = squared * lax.rsqrt(squared)
                inside = jnp.maximum(4.0 - ratio, 0.0)
                fourth = inside * inside
                value = (fourth * fourth) * (5.0 - inside)
                for side in range(2):
                    hi, lo = split2(value[:, side * LANES : (side + 1) * LANES])
                    k_hi[left // LANES + side, target, :] = hi
                    k_lo[left // LANES + side, target, :] = lo

    def build_lattice(panel, carry):
        at = pl.ds(pl.multiple_of(panel * LANES, LANES), LANES)
        index, weight = ffd_index_ref[:, at], ffd_weight_ref[:, at]
        slots = index.shape[0]
        slot = lax.broadcasted_iota(jnp.int32, index.shape, 0)
        total, repeat = weight, jnp.zeros(index.shape, jnp.int32)
        for turn in range(1, slots):
            same = pltpu.roll(index, turn, 0) == index
            total = total + jnp.where(same, pltpu.roll(weight, turn, 0), 0.0)
            repeat = jnp.where(jnp.logical_and(same, slot >= turn), 1, repeat)
        index = jnp.where(repeat == 1, -1, index)
        hi = total.astype(jnp.bfloat16).astype(jnp.float32)
        lo = total - hi
        tall = (2 * ROWS, LANES)

        def spread(value, kind):
            return [jnp.broadcast_to(value[s : s + 1], tall).astype(kind) for s in range(slots)]

        index, hi, lo = spread(index, jnp.int16), spread(hi, jnp.bfloat16), spread(lo, jnp.bfloat16)
        row = lax.broadcasted_iota(jnp.int32, tall, 0).astype(jnp.int16)
        for column in range(0, FFD, LANES):
            rows_hi, rows_lo = [], []
            for top in range(column, column + LANES, 2 * ROWS):
                found_hi = found_lo = jnp.zeros(tall, jnp.bfloat16)
                here_row = row + jnp.int16(top)
                for s in range(slots):
                    match = index[s] == here_row
                    found_hi = jnp.where(match, hi[s], found_hi)
                    found_lo = jnp.where(match, lo[s], found_lo)
                rows_hi.append(found_hi)
                rows_lo.append(found_lo)
            l_hi[column // LANES, at, :] = jnp.concatenate(rows_hi, axis=0).T
            l_lo[column // LANES, at, :] = jnp.concatenate(rows_lo, axis=0).T
        return carry

    pieces, stride = rows // ROWS, ROWS // nodes_here
    zero = jnp.zeros((ROWS, LANES), jnp.float32)

    def arrives_late(piece, chunk, far_low, far_high):
        first_row = chunk + stride * piece
        last_row = first_row + stride - 1
        return (far_low and first_row < blocks) or (far_high and last_row >= 2 * blocks)

    def seek(sweep, face, piece, found, chunks):
        span = slice(piece * ROWS, (piece + 1) * ROWS)
        rel, lane = rel_ref[face, span, :], lane_ref[face, span, :]
        for chunk in chunks:
            match = rel == chunk
            at = (chunk + stride * piece) * nodes_here
            for comp in range(5):
                window = wide[sweep, comp, at : at + ROWS, :]
                taken = jnp.take_along_axis(window, lane, axis=1)
                found[comp] = jnp.where(match, taken, found[comp])
        return found

    def chunk_lists(piece, far):
        late = [c for c in range(2 * blocks + 1) if arrives_late(piece, c, *far)]
        return [c for c in range(2 * blocks + 1) if c not in late], late

    def relax_early(sweep, far):
        for face in range(off_ref.shape[0]):
            for piece in range(pieces):
                found = seek(sweep, face, piece, [zero] * 5, chunk_lists(piece, far)[0])
                for comp in range(5):
                    found_ref[face, piece, comp] = found[comp]

    def relax_late(sweep, far):
        for piece in range(pieces):
            span = slice(piece * ROWS, (piece + 1) * ROWS)
            coupled = [zero] * 5
            for face in range(off_ref.shape[0]):
                found = [found_ref[face, piece, comp] for comp in range(5)]
                found = seek(sweep, face, piece, found, chunk_lists(piece, far)[1])
                for a in range(5):
                    for b in range(5):
                        block = off_ref[face, 5 * a + b, span].astype(jnp.float32)
                        coupled[a] = coupled[a] + block * found[b]
            rest = [rhs_ref[b, span] - coupled[b] for b in range(5)]
            for a in range(5):
                total = inv_ref[5 * a, span] * rest[0]
                for b in range(1, 5):
                    total = total + inv_ref[5 * a + b, span] * rest[b]
                if sweep + 1 < SWEEPS:
                    at = rows + piece * ROWS
                    wide[sweep + 1, a, at : at + ROWS, :] = total
                else:
                    out_ref[a, span] = total

    def by_side(work, sweep):
        for far in sorted({(s == 0, s == subs - 1) for s in range(subs)}):
            same = jnp.logical_and(
                (sub_at == 0) == far[0], (sub_at == subs - 1) == far[1]
            )
            pl.when(same)(functools.partial(work, sweep, far))

    def halo_near(sweep):
        @pl.when(sub_at > 0)
        def _():
            halo(sweep, 0).wait_recv()

        @pl.when(sub_at < subs - 1)
        def _():
            halo(sweep, 1).wait_recv()

    def halo_far(sweep):
        @pl.when(jnp.logical_and(sub_at == 0, here > 0))
        def _():
            halo(sweep, 0).wait_recv()

        @pl.when(jnp.logical_and(sub_at == subs - 1, here < places - 1))
        def _():
            halo(sweep, 1).wait_recv()

    panel_pairs = base_own // width
    second_cut, third_cut = ((panel_pairs * part // 4) * width for part in (2, 3))

    def early_with(step, begin, end):
        def work(sweep, far):
            build_kernel(step, begin, end)
            relax_early(sweep, far)

        return work

    build_features(0)
    build_kernel(0, 0, second_cut)
    halo_near(0)
    by_side(early_with(0, second_cut, third_cut), 0)
    pass_on()
    load_wait(4, 5)
    halo_far(0)
    by_side(relax_late, 0)
    halo_start(1)
    crew_known()
    tell(0)
    build_kernel(0, third_cut, base_own)
    for step in range(1, subs):
        point_copy(step).wait_recv()
        build_features(step)
        if step < subs - 1:
            build_kernel(step, 0, base_own)
    load_wait(6, 7, 8)
    halo_near(1)
    by_side(early_with(subs - 1, 0, second_cut if subs > 1 else 0), 1)
    halo_far(1)
    by_side(relax_late, 1)
    for k in range(3):
        total = out_ref[0] * sens_ref[k].astype(jnp.float32)
        for a in range(1, 5):
            total = total + out_ref[a] * sens_ref[3 * a + k].astype(jnp.float32)
        sens_rows[k] = total
    for k in range(3):
        total = weight_ref[0] * sens_rows[k, pl.ds(0, blocks, stride=nodes_here), :]
        for n in range(1, nodes_here):
            total = total + weight_ref[n] * sens_rows[k, pl.ds(n, blocks, stride=nodes_here), :]
        sens_slots[team, k] = total

    def sens_copy(node_step, sub_step):
        return pltpu.make_async_remote_copy(
            src_ref=sens_slots.at[team],
            dst_ref=sens_slots.at[team],
            send_sem=sens_send,
            recv_sem=sens_recv,
            device_id={
                "nodes": (node_at + node_step) % nodes,
                "sub": (sub_at + sub_step) % subs,
            },
            device_id_type=MESH,
        )

    crew_steps = [(n, s) for n in range(1, nodes) for s in range(subs)]
    crew_steps += [(0, s) for s in range(1, subs)]
    for node_step, sub_step in crew_steps:
        sens_copy(node_step, sub_step).start()
    if cells > 2:
        hear(0)
        tell(1)
    sens_mat[...] = jnp.zeros_like(sens_mat)
    if subs > 1:
        build_kernel(subs - 1, second_cut, base_own)
    for stage in range(2, cells - 1):
        hear(stage - 1)
        tell(stage)
    lax.fori_loop(0, panels, build_lattice, 0)
    arrive(sens_slots.at[pl.ds(0, crew - 1)], sens_recv)
    for step in range(subs):
        whose = (sub_at - step + subs) % subs
        for k in range(3):
            total = sens_slots[whose, k]
            for n in range(1, nodes):
                total = total + sens_slots[n * subs + whose, k]
            hi = total.astype(jnp.bfloat16).astype(jnp.float32)
            lo = total - hi
            for block in range(blocks):
                at = step * cell_count + block * LANES
                sens_mat[k : k + 1, at : at + LANES] = hi[block : block + 1, :]
                sens_mat[ROWS + k : ROWS + k + 1, at : at + LANES] = lo[block : block + 1, :]

    left = sens_mat[...].astype(jnp.bfloat16)
    pieces_hi, pieces_lo = [], []
    for pair in range(0, panels, 2):
        product = jnp.zeros((2 * ROWS, 2 * LANES), jnp.float32)
        for table in (k_hi, k_lo):
            both = jnp.concatenate([table[pair], table[pair + 1]], axis=1)
            product = product + jnp.dot(left, both, preferred_element_type=jnp.float32)
        base_grad = (product[0:ROWS] + product[ROWS:]) * scale
        hi = base_grad.astype(jnp.bfloat16).astype(jnp.float32)
        pieces_hi.append(hi)
        pieces_lo.append(base_grad - hi)
    left = jnp.concatenate(
        [jnp.concatenate(pieces_hi, axis=1), jnp.concatenate(pieces_lo, axis=1)], axis=0
    ).astype(jnp.bfloat16)
    owns = []
    for pair in range(0, FFD // LANES, 2):
        product = jnp.zeros((2 * ROWS, 2 * LANES), jnp.float32)
        for table in (l_hi, l_lo):
            both = jnp.concatenate([table[pair], table[pair + 1]], axis=1)
            product = product + jnp.dot(left, both, preferred_element_type=jnp.float32)
        owns.append(product[0:ROWS] + product[ROWS:])
    own = jnp.concatenate(owns, axis=1)
    for block in range(FFD // LANES):
        grad_slots[me, 3 * block : 3 * block + 3, :] = own[
            0:3, block * LANES : (block + 1) * LANES
        ]

    def grad_copy(slot):
        return pltpu.make_async_remote_copy(
            src_ref=grad_slots.at[me],
            dst_ref=grad_slots.at[me],
            send_sem=grad_send,
            recv_sem=grad_recv,
            device_id={
                "cells": slot // crew,
                "nodes": slot % crew // subs,
                "sub": slot % subs,
            },
            device_id_type=MESH,
        )

    if cells > 1:
        hear(cells - 2)
    for slot in range(everyone):
        pl.when(slot != me)(grad_copy(slot).start)
    halo_sent()
    for step in range(1, subs):
        point_copy(step).wait_send()
    arrive(sens_slots.at[pl.ds(0, crew - 1)], sens_send)
    others = grad_slots.at[pl.ds(0, everyone - 1)]
    arrive(others, grad_send)
    arrive(others, grad_recv)
    total = grad_slots[0]
    for slot in range(1, everyone):
        total = total + grad_slots[slot]
    for block in range(FFD // LANES):
        grad_ref[:, block * LANES : (block + 1) * LANES] = total[3 * block : 3 * block + 3, :]


def finish(adjoint_in, control_in, adjoint_out, control_out):
    adjoint_out[...] = adjoint_in[...]
    control_out[...] = control_in[...]


def to_rows(array):
    array = jnp.moveaxis(array, 0, -2)
    lead, (nodes, cells) = array.shape[:-2], array.shape[-2:]
    array = array.reshape(lead + (nodes, cells // LANES, LANES))
    array = jnp.swapaxes(array, -3, -2)
    return array.reshape(lead + (nodes * cells // LANES, LANES))


def from_rows(array, nodes):
    lead, rows = array.shape[:-2], array.shape[-2]
    array = array.reshape(lead + (rows // nodes, nodes, LANES))
    array = jnp.swapaxes(array, -3, -2).reshape(lead + (nodes, rows // nodes * LANES))
    return jnp.moveaxis(array, -2, 0)


def body(
    adjoint_start,
    adjoint_rhs,
    off_blocks,
    diag_inverse,
    neighbours,
    node_weights,
    sens_blocks,
    cell_points,
    base_points,
    ffd_index,
    ffd_weight,
):
    nodes_here, _, cell_count = adjoint_start.shape
    faces = off_blocks.shape[1]
    cells, subs, nodes = (lax.axis_size(a) for a in ("cells", "sub", "nodes"))
    crew = nodes * subs
    everyone = cells * crew
    blocks = cell_count // LANES
    rows = blocks * nodes_here
    base_own = base_points.shape[1] // crew
    panels = base_own // LANES
    scale = 1.0 / 256.0 / float(cell_count * cells * subs) ** 0.5
    vmem = pl.BlockSpec(memory_space=pltpu.VMEM)
    hbm = pl.BlockSpec(memory_space=pltpu.HBM)
    f32, bf16 = jnp.float32, jnp.bfloat16
    dma = pltpu.SemaphoreType.DMA
    off_rows, inv_rows = to_rows(off_blocks), to_rows(diag_inverse)
    sens_cells = to_rows(sens_blocks)
    adjoint, control = pl.pallas_call(
        functools.partial(kernel, scale),
        out_shape=(
            jax.ShapeDtypeStruct((5, rows, LANES), f32),
            jax.ShapeDtypeStruct((3, FFD), f32),
        ),
        in_specs=[hbm] * 11,
        out_specs=(vmem, vmem),
        scratch_shapes=[
            pltpu.SMEM(node_weights.shape, f32),
            pltpu.VMEM(cell_points.shape, f32),
            pltpu.VMEM(neighbours.shape, jnp.int32),
            pltpu.VMEM((3, base_own), f32),
            pltpu.VMEM(off_rows.shape, bf16),
            pltpu.VMEM((5, rows, LANES), f32),
            pltpu.VMEM(inv_rows.shape, f32),
            pltpu.VMEM(sens_cells.shape, bf16),
            pltpu.VMEM((ffd_index.shape[1], base_own), jnp.int32),
            pltpu.VMEM((ffd_index.shape[1], base_own), f32),
            pltpu.VMEM((SWEEPS, 5, 3 * rows, LANES), f32),
            pltpu.VMEM((faces, rows, LANES), jnp.int32),
            pltpu.VMEM((faces, rows, LANES), jnp.int32),
            pltpu.VMEM((faces, rows // ROWS, 5, ROWS, LANES), f32),
            pltpu.VMEM((subs, 3, cell_count), f32),
            pltpu.VMEM((cell_count, 24), bf16),
            pltpu.VMEM((24, max(cell_count, base_own)), f32),
            pltpu.VMEM((24, base_own), bf16),
            pltpu.VMEM((panels, subs * cell_count, LANES), bf16),
            pltpu.VMEM((panels, subs * cell_count, LANES), bf16),
            pltpu.VMEM((FFD // LANES, base_own, LANES), bf16),
            pltpu.VMEM((FFD // LANES, base_own, LANES), bf16),
            pltpu.VMEM((3, rows, LANES), f32),
            pltpu.VMEM((crew, 3, blocks, LANES), f32),
            pltpu.VMEM((2 * ROWS, subs * cell_count), f32),
            pltpu.VMEM((everyone, 3 * FFD // LANES, LANES), f32),
            dma((9,)),
            dma((2,)),
            dma((SWEEPS, 2)),
            dma((max(subs - 1, 1),)),
            dma((max(subs - 1, 1),)),
            dma,
            dma,
            dma,
            dma,
            pltpu.SemaphoreType.REGULAR((max(cells - 1, 1),)),
            pltpu.SemaphoreType.REGULAR((2,)),
        ],
        compiler_params=pltpu.CompilerParams(
            collective_id=0, has_side_effects=True, vmem_limit_bytes=16 * 1024 * 1024
        ),
    )(
        *(pltpu.with_memory_space_constraint(array, pltpu.HBM) for array in (
            node_weights,
            to_rows(adjoint_start),
            cell_points,
            neighbours,
            base_points,
            off_rows,
            to_rows(adjoint_rhs),
            inv_rows,
            sens_cells,
            ffd_index.T,
            ffd_weight.T,
        ))
    )
    adjoint, control = pl.pallas_call(
        finish,
        out_shape=(
            jax.ShapeDtypeStruct((5, rows, LANES), f32),
            jax.ShapeDtypeStruct((3, FFD), f32),
        ),
        in_specs=[vmem] * 2,
        out_specs=(vmem, vmem),
        compiler_params=pltpu.CompilerParams(vmem_limit_bytes=1024 * 1024),
    )(adjoint, control)
    return from_rows(adjoint, nodes_here), control


def solution(mesh):
    return jax.shard_map(
        body,
        mesh=mesh,
        in_specs=(
            P("nodes", None, ("groups", "cells", "sub")),
            P("nodes", None, ("groups", "cells", "sub")),
            P("nodes", None, None, ("groups", "cells", "sub")),
            P("nodes", None, ("groups", "cells", "sub")),
            P(None, ("cells", "sub")),
            P("nodes"),
            P("nodes", None, ("groups", "cells", "sub")),
            P(None, ("cells", "sub")),
            P(),
            P(),
            P(),
        ),
        out_specs=(P("nodes", None, ("groups", "cells", "sub")), P("groups", None)),
        check_vma=False,
    )
```

```python
import functools

import jax
import jax.numpy as jnp
from jax import lax
from jax.experimental import pallas as pl
from jax.experimental.pallas import tpu as pltpu
from jax.sharding import PartitionSpec as P

SWEEPS = 2
FFD = 512
LANES = 128
ROWS = 8
PIECE = 64

support_radius = 0.3
MESH = pl.DeviceIdType.MESH


def split2(x):
    hi = x.astype(jnp.bfloat16)
    return hi, (x - hi.astype(jnp.float32)).astype(jnp.bfloat16)


def split3(x):
    one = x.astype(jnp.bfloat16).astype(jnp.float32)
    two = (x - one).astype(jnp.bfloat16).astype(jnp.float32)
    return one, two, (x - one) - two


def kernel(
    scale,
    weight_hbm,
    adj_hbm,
    point_hbm,
    nb_hbm,
    base_hbm,
    off_hbm,
    rhs_hbm,
    inv_hbm,
    sens_hbm,
    ffd_index_hbm,
    ffd_weight_hbm,
    out_ref,
    grad_ref,
    weight_ref,
    point_ref,
    nb_ref,
    base_ref,
    off_ref,
    rhs_ref,
    inv_ref,
    sens_ref,
    ffd_index_ref,
    ffd_weight_ref,
    wide,
    rel_ref,
    lane_ref,
    found_ref,
    points,
    cell_rows,
    cell_feat,
    base_feat,
    k_hi,
    k_lo,
    l_hi,
    l_lo,
    sens_rows,
    sens_slots,
    sens_mat,
    grad_slots,
    load_sem,
    halo_send,
    halo_recv,
    point_send,
    point_recv,
    sens_send,
    sens_recv,
    grad_send,
    grad_recv,
    known,
    met,
):
    cells, subs, nodes = (lax.axis_size(a) for a in ("cells", "sub", "nodes"))
    cell_at, sub_at, node_at = (lax.axis_index(a) for a in ("cells", "sub", "nodes"))
    here, places = cell_at * subs + sub_at, cells * subs
    team, crew = node_at * subs + sub_at, nodes * subs
    me, everyone = cell_at * crew + team, cells * crew
    nodes_here = weight_ref.shape[0]
    rows = adj_hbm.shape[1]
    blocks = rows // nodes_here
    cell_count = blocks * LANES
    base_own = base_ref.shape[1]
    panels = base_own // LANES

    lower, upper = cell_at > 0, cell_at < cells - 1
    below, above = cell_at - 1, cell_at + 1
    beside_count = lower.astype(jnp.int32) + upper.astype(jnp.int32)

    adj_load = pltpu.make_async_copy(
        adj_hbm, wide.at[0, :, pl.ds(rows, rows), :], load_sem.at[0]
    )
    adj_load.start()
    barrier = pltpu.get_barrier_semaphore()

    def greet(device):
        pl.semaphore_signal(barrier, inc=1, device_id=device, device_id_type=MESH)

    first, last = sub_at == 0, sub_at == subs - 1
    down, up = jnp.logical_and(lower, first), jnp.logical_and(upper, last)
    abroad = [(last, {"nodes": (node_at + step) % nodes}) for step in range(1, nodes)]
    abroad += [(down, {"cells": below, "sub": subs - 1}), (up, {"cells": above, "sub": 0})]
    greeted = jnp.int32(subs - 1)
    for exists, device in abroad:
        pl.when(exists)(functools.partial(greet, device))
        greeted = greeted + exists.astype(jnp.int32)
    for step in range(1, subs):
        greet({"sub": (sub_at + step) % subs})

    base_start = pl.multiple_of(team * base_own, LANES)
    share = pl.ds(base_start, base_own)
    sources = (
        (0, adj_hbm, wide.at[0, :, pl.ds(rows, rows), :]),
        (1, point_hbm, point_ref),
        (2, base_hbm.at[:, share], base_ref),
        (3, nb_hbm, nb_ref),
        (4, off_hbm, off_ref),
        (5, rhs_hbm, rhs_ref),
        (5, inv_hbm, inv_ref),
        (6, sens_hbm, sens_ref),
        (7, ffd_index_hbm.at[:, share], ffd_index_ref),
        (7, ffd_weight_hbm.at[:, share], ffd_weight_ref),
        (8, weight_hbm, weight_ref),
    )
    for group, source, target in sources[1:]:
        pltpu.make_async_copy(source, target, load_sem.at[group]).start()

    def arrive(size, sem):
        pltpu.make_async_copy(size, size, sem).wait()

    sizes = [source[2] for source in sources if source[0] not in (5, 7)]
    sizes.insert(5, wide)
    sizes.insert(7, cell_feat.at[0 : 2 * ffd_index_ref.shape[0], 0:base_own])

    def load_wait(*groups):
        for group in groups:
            arrive(sizes[group], load_sem.at[group])

    def tell(stage):
        for exists, other in ((upper, above), (lower, below)):

            @pl.when(exists)
            def _():
                pl.semaphore_signal(
                    known.at[stage],
                    inc=1,
                    device_id={"cells": other},
                    device_id_type=MESH,
                )

    def hear(stage):
        pl.semaphore_wait(known.at[stage], beside_count)

    def meet(which, device):
        pl.semaphore_signal(met.at[which], inc=1, device_id=device, device_id_type=MESH)

    def announce():
        for exists, device in abroad:
            pl.when(exists)(functools.partial(meet, 0, device))

    def pass_on():
        expected = greeted - (subs - 1)

        @pl.when(expected > 0)
        def _():
            pl.semaphore_wait(met.at[0], expected)

        @pl.when(jnp.logical_or(first, last))
        def _():
            for step in range(1, subs):
                meet(1, {"sub": (sub_at + step) % subs})

    def crew_known():
        if subs > 1:
            others = (sub_at != 0).astype(jnp.int32) + (sub_at != subs - 1).astype(jnp.int32)
            pl.semaphore_wait(met.at[1], others)

    @pl.when(here == 0)
    def _():
        wide[:, :, 0:rows, :] = jnp.zeros((SWEEPS, 5, rows, LANES), jnp.float32)

    @pl.when(here == places - 1)
    def _():
        wide[:, :, 2 * rows : 3 * rows, :] = jnp.zeros((SWEEPS, 5, rows, LANES), jnp.float32)

    def halo(sweep, side, top=0, tall=rows):
        other = here + 1 if side == 0 else here - 1
        start = 0 if side == 0 else 2 * rows
        return pltpu.make_async_remote_copy(
            src_ref=wide.at[sweep, :, pl.ds(rows + top, tall), :],
            dst_ref=wide.at[sweep, :, pl.ds(start + top, tall), :],
            send_sem=halo_send.at[side],
            recv_sem=halo_recv.at[sweep, side],
            device_id={"cells": other // subs, "sub": other % subs},
            device_id_type=MESH,
        )

    def halo_start(sweep, top, tall):
        for side, exists in enumerate((here < places - 1, here > 0)):

            @pl.when(exists)
            def _():
                halo(sweep, side, top, tall).start()

    def halo_sent():
        both = wide.at[:, :, pl.ds(rows, rows), :]

        @pl.when(here < places - 1)
        def _():
            arrive(both, halo_send.at[0])

        @pl.when(here > 0)
        def _():
            arrive(both, halo_send.at[1])

    def point_copy(step):
        return pltpu.make_async_remote_copy(
            src_ref=point_ref,
            dst_ref=points.at[step],
            send_sem=point_send.at[step - 1],
            recv_sem=point_recv.at[step - 1],
            device_id={"sub": (sub_at + step) % subs},
            device_id_type=MESH,
        )

    load_wait(0, 1)
    pl.semaphore_wait(barrier, greeted)
    halo_start(0, 0, rows)
    for step in range(1, subs):
        point_copy(step).start()
    announce()

    load_wait(2, 3)
    first_cell = here * cell_count
    for face in range(nb_ref.shape[0]):
        for block in range(blocks):
            entry = nb_ref[face : face + 1, block * LANES : (block + 1) * LANES]
            local = entry - first_cell + cell_count
            chunk = jnp.where(entry >= 0, (local >> 7) - block, -1)
            span = pl.ds(block * nodes_here, nodes_here)
            rel_ref[face, span, :] = jnp.broadcast_to(chunk, (nodes_here, LANES))
            lane_ref[face, span, :] = jnp.broadcast_to(local & (LANES - 1), (nodes_here, LANES))

    def features(xyz, own):
        one, two, three = split3(xyz)
        square = xyz[0:1] * xyz[0:1] + xyz[1:2] * xyz[1:2] + xyz[2:3] * xyz[2:3]
        pieces = [one, one, two, two, one, three] if own else [one, two, one, two, three, one]
        parts = split3(square)
        ones = jnp.ones_like(square)
        for slot, piece in enumerate(pieces):
            cell_feat[3 * slot : 3 * slot + 3, 0 : xyz.shape[1]] = piece if own else -2.0 * piece
        for slot in range(3):
            cell_feat[18 + slot : 19 + slot, 0 : xyz.shape[1]] = parts[slot] if own else ones
            cell_feat[21 + slot : 22 + slot, 0 : xyz.shape[1]] = ones if own else parts[slot]

    stretch = 4.0 / support_radius
    features((base_ref[...] - 0.5) * stretch, False)
    base_feat[...] = cell_feat[:, 0:base_own].astype(jnp.bfloat16)

    def build_features(step):
        xyz = point_ref[...] if step == 0 else points[step]
        features((xyz - 0.5) * stretch, True)
        cell_rows[step] = cell_feat[:, 0:cell_count].T.astype(jnp.bfloat16)

    width = 2 * LANES

    def build_kernel(step, begin, end):
        for left in range(begin, end, width):
            other = base_feat[:, left : left + width]
            for top in range(0, cell_count, PIECE):
                mine = cell_rows[step, top : top + PIECE, :]
                target = slice(step * cell_count + top, step * cell_count + top + PIECE)
                squared = jnp.dot(mine, other, preferred_element_type=jnp.float32)
                squared = jnp.maximum(squared, 1e-20)
                ratio = squared * lax.rsqrt(squared)
                inside = jnp.maximum(4.0 - ratio, 0.0)
                fourth = inside * inside
                value = (fourth * fourth) * (5.0 - inside)
                for side in range(2):
                    hi, lo = split2(value[:, side * LANES : (side + 1) * LANES])
                    k_hi[left // LANES + side, target, :] = hi
                    k_lo[left // LANES + side, target, :] = lo

    def build_lattice(panel):
        at = slice(panel * LANES, (panel + 1) * LANES)
        index, weight = ffd_index_ref[:, at], ffd_weight_ref[:, at]
        slots = index.shape[0]
        slot = lax.broadcasted_iota(jnp.int32, index.shape, 0)
        total, repeat = weight, jnp.zeros(index.shape, jnp.int32)
        for turn in range(1, slots):
            same = pltpu.roll(index, turn, 0) == index
            total = total + jnp.where(same, pltpu.roll(weight, turn, 0), 0.0)
            repeat = jnp.where(jnp.logical_and(same, slot >= turn), 1, repeat)
        index = jnp.where(repeat == 1, -1, index)
        hi = total.astype(jnp.bfloat16).astype(jnp.float32)
        lo = total - hi
        tall = (2 * ROWS, LANES)

        def spread(value, kind):
            return [jnp.broadcast_to(value[s : s + 1], tall).astype(kind) for s in range(slots)]

        index, hi, lo = spread(index, jnp.int16), spread(hi, jnp.bfloat16), spread(lo, jnp.bfloat16)
        row = lax.broadcasted_iota(jnp.int32, tall, 0).astype(jnp.int16)
        for column in range(0, FFD, LANES):
            rows_hi, rows_lo = [], []
            for top in range(column, column + LANES, 2 * ROWS):
                found_hi = found_lo = jnp.zeros(tall, jnp.bfloat16)
                here_row = row + jnp.int16(top)
                for s in range(slots):
                    match = index[s] == here_row
                    found_hi = jnp.where(match, hi[s], found_hi)
                    found_lo = jnp.where(match, lo[s], found_lo)
                rows_hi.append(found_hi)
                rows_lo.append(found_lo)
            l_hi[column // LANES, at, :] = jnp.concatenate(rows_hi, axis=0).T
            l_lo[column // LANES, at, :] = jnp.concatenate(rows_lo, axis=0).T

    pieces, stride = rows // ROWS, ROWS // nodes_here
    zero = jnp.zeros((ROWS, LANES), jnp.float32)

    def arrives_late(piece, chunk, far_low, far_high):
        first_row = chunk + stride * piece
        last_row = first_row + stride - 1
        return (far_low and first_row < blocks) or (far_high and last_row >= 2 * blocks)

    def seek(sweep, face, piece, found, chunks):
        span = slice(piece * ROWS, (piece + 1) * ROWS)
        rel, lane = rel_ref[face, span, :], lane_ref[face, span, :]
        for chunk in chunks:
            match = rel == chunk
            at = (chunk + stride * piece) * nodes_here
            for comp in range(5):
                window = wide[sweep, comp, at : at + ROWS, :]
                taken = jnp.take_along_axis(window, lane, axis=1)
                found[comp] = jnp.where(match, taken, found[comp])
        return found

    def chunk_lists(piece, far):
        late = [c for c in range(2 * blocks + 1) if arrives_late(piece, c, *far)]
        return [c for c in range(2 * blocks + 1) if c not in late], late

    def relax_early(sweep, far):
        for face in range(off_ref.shape[0]):
            for piece in range(pieces):
                found = seek(sweep, face, piece, [zero] * 5, chunk_lists(piece, far)[0])
                for comp in range(5):
                    found_ref[face, piece, comp] = found[comp]

    def relax_late(sweep, far):
        for piece in range(pieces):
            span = slice(piece * ROWS, (piece + 1) * ROWS)
            coupled = [zero] * 5
            for face in range(off_ref.shape[0]):
                found = [found_ref[face, piece, comp] for comp in range(5)]
                found = seek(sweep, face, piece, found, chunk_lists(piece, far)[1])
                for a in range(5):
                    for b in range(5):
                        block = off_ref[face, 5 * a + b, span].astype(jnp.float32)
                        coupled[a] = coupled[a] + block * found[b]
            rest = [rhs_ref[b, span] - coupled[b] for b in range(5)]
            for a in range(5):
                total = inv_ref[5 * a, span] * rest[0]
                for b in range(1, 5):
                    total = total + inv_ref[5 * a + b, span] * rest[b]
                if sweep + 1 < SWEEPS:
                    at = rows + piece * ROWS
                    wide[sweep + 1, a, at : at + ROWS, :] = total
                else:
                    out_ref[a, span] = total
            if sweep + 1 < SWEEPS:
                halo_start(sweep + 1, piece * ROWS, ROWS)

    def by_side(work, sweep):
        for far in sorted({(s == 0, s == subs - 1) for s in range(subs)}):
            same = jnp.logical_and(
                (sub_at == 0) == far[0], (sub_at == subs - 1) == far[1]
            )
            pl.when(same)(functools.partial(work, sweep, far))

    def halo_near(sweep):
        @pl.when(sub_at > 0)
        def _():
            halo(sweep, 0).wait_recv()

        @pl.when(sub_at < subs - 1)
        def _():
            halo(sweep, 1).wait_recv()

    def halo_far(sweep):
        @pl.when(jnp.logical_and(sub_at == 0, here > 0))
        def _():
            halo(sweep, 0).wait_recv()

        @pl.when(jnp.logical_and(sub_at == subs - 1, here < places - 1))
        def _():
            halo(sweep, 1).wait_recv()

    panel_pairs = base_own // width
    second_cut, third_cut = ((panel_pairs * part // 4) * width for part in (2, 3))

    def early_with(step, begin, end):
        def work(sweep, far):
            build_kernel(step, begin, end)
            relax_early(sweep, far)

        return work

    build_features(0)
    build_kernel(0, 0, second_cut)
    halo_near(0)
    by_side(early_with(0, second_cut, third_cut), 0)
    pass_on()
    load_wait(4, 5)
    halo_far(0)
    by_side(relax_late, 0)
    crew_known()
    tell(0)
    for step in range(1, subs):
        point_copy(step).wait_recv()
        build_features(step)
    build_kernel(0, third_cut, base_own)
    for step in range(1, subs - 1):
        build_kernel(step, 0, base_own)
    load_wait(6, 7, 8)
    halo_near(1)
    by_side(early_with(subs - 1, 0, second_cut if subs > 1 else 0), 1)
    halo_far(1)
    by_side(relax_late, 1)
    for k in range(3):
        total = out_ref[0] * sens_ref[k].astype(jnp.float32)
        for a in range(1, 5):
            total = total + out_ref[a] * sens_ref[3 * a + k].astype(jnp.float32)
        sens_rows[k] = total
    for k in range(3):
        total = weight_ref[0] * sens_rows[k, pl.ds(0, blocks, stride=nodes_here), :]
        for n in range(1, nodes_here):
            total = total + weight_ref[n] * sens_rows[k, pl.ds(n, blocks, stride=nodes_here), :]
        sens_slots[team, k] = total

    def sens_copy(node_step, sub_step):
        return pltpu.make_async_remote_copy(
            src_ref=sens_slots.at[team],
            dst_ref=sens_slots.at[team],
            send_sem=sens_send,
            recv_sem=sens_recv,
            device_id={
                "nodes": (node_at + node_step) % nodes,
                "sub": (sub_at + sub_step) % subs,
            },
            device_id_type=MESH,
        )

    crew_steps = [(n, s) for n in range(1, nodes) for s in range(subs)]
    crew_steps += [(0, s) for s in range(1, subs)]
    for node_step, sub_step in crew_steps:
        sens_copy(node_step, sub_step).start()
    if cells > 2:
        hear(0)
        tell(1)
    sens_mat[...] = jnp.zeros_like(sens_mat)
    if subs > 1:
        build_kernel(subs - 1, second_cut, base_own)
    for panel in range(panels):
        build_lattice(panel)
    for stage in range(2, cells - 1):
        hear(stage - 1)
        tell(stage)
    arrive(sens_slots.at[pl.ds(0, crew - 1)], sens_recv)
    for step in range(subs):
        whose = (sub_at - step + subs) % subs
        for k in range(3):
            total = sens_slots[whose, k]
            for n in range(1, nodes):
                total = total + sens_slots[n * subs + whose, k]
            hi = total.astype(jnp.bfloat16).astype(jnp.float32)
            lo = total - hi
            for block in range(blocks):
                at = step * cell_count + block * LANES
                sens_mat[k : k + 1, at : at + LANES] = hi[block : block + 1, :]
                sens_mat[ROWS + k : ROWS + k + 1, at : at + LANES] = lo[block : block + 1, :]

    left = sens_mat[...].astype(jnp.bfloat16)
    pieces_hi, pieces_lo = [], []
    for pair in range(0, panels, 2):
        product = jnp.zeros((2 * ROWS, 2 * LANES), jnp.float32)
        for table in (k_hi, k_lo):
            both = jnp.concatenate([table[pair], table[pair + 1]], axis=1)
            product = product + jnp.dot(left, both, preferred_element_type=jnp.float32)
        base_grad = (product[0:ROWS] + product[ROWS:]) * scale
        hi = base_grad.astype(jnp.bfloat16).astype(jnp.float32)
        pieces_hi.append(hi)
        pieces_lo.append(base_grad - hi)
    left = jnp.concatenate(
        [jnp.concatenate(pieces_hi, axis=1), jnp.concatenate(pieces_lo, axis=1)], axis=0
    ).astype(jnp.bfloat16)
    owns = []
    for pair in range(0, FFD // LANES, 2):
        product = jnp.zeros((2 * ROWS, 2 * LANES), jnp.float32)
        for table in (l_hi, l_lo):
            both = jnp.concatenate([table[pair], table[pair + 1]], axis=1)
            product = product + jnp.dot(left, both, preferred_element_type=jnp.float32)
        owns.append(product[0:ROWS] + product[ROWS:])
    own = jnp.concatenate(owns, axis=1)
    for block in range(FFD // LANES):
        grad_slots[me, 3 * block : 3 * block + 3, :] = own[
            0:3, block * LANES : (block + 1) * LANES
        ]

    def grad_copy(slot):
        return pltpu.make_async_remote_copy(
            src_ref=grad_slots.at[me],
            dst_ref=grad_slots.at[me],
            send_sem=grad_send,
            recv_sem=grad_recv,
            device_id={
                "cells": slot // crew,
                "nodes": slot % crew // subs,
                "sub": slot % subs,
            },
            device_id_type=MESH,
        )

    if cells > 1:
        hear(cells - 2)
    for slot in range(everyone):
        pl.when(slot != me)(grad_copy(slot).start)
    halo_sent()
    for step in range(1, subs):
        point_copy(step).wait_send()
    arrive(sens_slots.at[pl.ds(0, crew - 1)], sens_send)
    others = grad_slots.at[pl.ds(0, everyone - 1)]
    arrive(others, grad_send)
    arrive(others, grad_recv)
    total = grad_slots[0]
    for slot in range(1, everyone):
        total = total + grad_slots[slot]
    for block in range(FFD // LANES):
        grad_ref[:, block * LANES : (block + 1) * LANES] = total[3 * block : 3 * block + 3, :]


def finish(adjoint_in, control_in, adjoint_out, control_out):
    adjoint_out[...] = adjoint_in[...]
    control_out[...] = control_in[...]


def to_rows(array):
    array = jnp.moveaxis(array, 0, -2)
    lead, (nodes, cells) = array.shape[:-2], array.shape[-2:]
    array = array.reshape(lead + (nodes, cells // LANES, LANES))
    array = jnp.swapaxes(array, -3, -2)
    return array.reshape(lead + (nodes * cells // LANES, LANES))


def from_rows(array, nodes):
    lead, rows = array.shape[:-2], array.shape[-2]
    array = array.reshape(lead + (rows // nodes, nodes, LANES))
    array = jnp.swapaxes(array, -3, -2).reshape(lead + (nodes, rows // nodes * LANES))
    return jnp.moveaxis(array, -2, 0)


def body(
    adjoint_start,
    adjoint_rhs,
    off_blocks,
    diag_inverse,
    neighbours,
    node_weights,
    sens_blocks,
    cell_points,
    base_points,
    ffd_index,
    ffd_weight,
):
    nodes_here, _, cell_count = adjoint_start.shape
    faces = off_blocks.shape[1]
    cells, subs, nodes = (lax.axis_size(a) for a in ("cells", "sub", "nodes"))
    crew = nodes * subs
    everyone = cells * crew
    blocks = cell_count // LANES
    rows = blocks * nodes_here
    base_own = base_points.shape[1] // crew
    panels = base_own // LANES
    scale = 1.0 / 256.0 / float(cell_count * cells * subs) ** 0.5
    vmem = pl.BlockSpec(memory_space=pltpu.VMEM)
    hbm = pl.BlockSpec(memory_space=pltpu.HBM)
    f32, bf16 = jnp.float32, jnp.bfloat16
    dma = pltpu.SemaphoreType.DMA
    off_rows, inv_rows = to_rows(off_blocks), to_rows(diag_inverse)
    sens_cells = to_rows(sens_blocks)
    adjoint, control = pl.pallas_call(
        functools.partial(kernel, scale),
        out_shape=(
            jax.ShapeDtypeStruct((5, rows, LANES), f32),
            jax.ShapeDtypeStruct((3, FFD), f32),
        ),
        in_specs=[hbm] * 11,
        out_specs=(vmem, vmem),
        scratch_shapes=[
            pltpu.SMEM(node_weights.shape, f32),
            pltpu.VMEM(cell_points.shape, f32),
            pltpu.VMEM(neighbours.shape, jnp.int32),
            pltpu.VMEM((3, base_own), f32),
            pltpu.VMEM(off_rows.shape, bf16),
            pltpu.VMEM((5, rows, LANES), f32),
            pltpu.VMEM(inv_rows.shape, f32),
            pltpu.VMEM(sens_cells.shape, bf16),
            pltpu.VMEM((ffd_index.shape[1], base_own), jnp.int32),
            pltpu.VMEM((ffd_index.shape[1], base_own), f32),
            pltpu.VMEM((SWEEPS, 5, 3 * rows, LANES), f32),
            pltpu.VMEM((faces, rows, LANES), jnp.int32),
            pltpu.VMEM((faces, rows, LANES), jnp.int32),
            pltpu.VMEM((faces, rows // ROWS, 5, ROWS, LANES), f32),
            pltpu.VMEM((subs, 3, cell_count), f32),
            pltpu.VMEM((subs, cell_count, 24), bf16),
            pltpu.VMEM((24, max(cell_count, base_own)), f32),
            pltpu.VMEM((24, base_own), bf16),
            pltpu.VMEM((panels, subs * cell_count, LANES), bf16),
            pltpu.VMEM((panels, subs * cell_count, LANES), bf16),
            pltpu.VMEM((FFD // LANES, base_own, LANES), bf16),
            pltpu.VMEM((FFD // LANES, base_own, LANES), bf16),
            pltpu.VMEM((3, rows, LANES), f32),
            pltpu.VMEM((crew, 3, blocks, LANES), f32),
            pltpu.VMEM((2 * ROWS, subs * cell_count), f32),
            pltpu.VMEM((everyone, 3 * FFD // LANES, LANES), f32),
            dma((9,)),
            dma((2,)),
            dma((SWEEPS, 2)),
            dma((max(subs - 1, 1),)),
            dma((max(subs - 1, 1),)),
            dma,
            dma,
            dma,
            dma,
            pltpu.SemaphoreType.REGULAR((max(cells - 1, 1),)),
            pltpu.SemaphoreType.REGULAR((2,)),
        ],
        compiler_params=pltpu.CompilerParams(
            collective_id=0, has_side_effects=True, vmem_limit_bytes=16 * 1024 * 1024
        ),
    )(
        *(pltpu.with_memory_space_constraint(array, pltpu.HBM) for array in (
            node_weights,
            to_rows(adjoint_start),
            cell_points,
            neighbours,
            base_points,
            off_rows,
            to_rows(adjoint_rhs),
            inv_rows,
            sens_cells,
            ffd_index.T,
            ffd_weight.T,
        ))
    )
    adjoint, control = pl.pallas_call(
        finish,
        out_shape=(
            jax.ShapeDtypeStruct((5, rows, LANES), f32),
            jax.ShapeDtypeStruct((3, FFD), f32),
        ),
        in_specs=[vmem] * 2,
        out_specs=(vmem, vmem),
        compiler_params=pltpu.CompilerParams(vmem_limit_bytes=1024 * 1024),
    )(adjoint, control)
    return from_rows(adjoint, nodes_here), control


def solution(mesh):
    return jax.shard_map(
        body,
        mesh=mesh,
        in_specs=(
            P("nodes", None, ("groups", "cells", "sub")),
            P("nodes", None, ("groups", "cells", "sub")),
            P("nodes", None, None, ("groups", "cells", "sub")),
            P("nodes", None, ("groups", "cells", "sub")),
            P(None, ("cells", "sub")),
            P("nodes"),
            P("nodes", None, ("groups", "cells", "sub")),
            P(None, ("cells", "sub")),
            P(),
            P(),
            P(),
        ),
        out_specs=(P("nodes", None, ("groups", "cells", "sub")), P("groups", None)),
        check_vma=False,
    )
```

```python
import functools

import jax
import jax.numpy as jnp
from jax import lax
from jax.experimental import pallas as pl
from jax.experimental.pallas import tpu as pltpu
from jax.sharding import PartitionSpec as P

SWEEPS = 2
FFD = 512
LANES = 128
ROWS = 8
PIECE = 64

support_radius = 0.3
MESH = pl.DeviceIdType.MESH


def split2(x):
    hi = x.astype(jnp.bfloat16)
    return hi, (x - hi.astype(jnp.float32)).astype(jnp.bfloat16)


def split3(x):
    one = x.astype(jnp.bfloat16).astype(jnp.float32)
    two = (x - one).astype(jnp.bfloat16).astype(jnp.float32)
    return one, two, (x - one) - two


def kernel(
    scale,
    weight_hbm,
    adj_hbm,
    point_hbm,
    nb_hbm,
    base_hbm,
    off_hbm,
    rhs_hbm,
    inv_hbm,
    sens_hbm,
    ffd_index_hbm,
    ffd_weight_hbm,
    out_ref,
    grad_ref,
    weight_ref,
    point_ref,
    nb_ref,
    base_ref,
    off_ref,
    rhs_ref,
    inv_ref,
    sens_ref,
    ffd_index_ref,
    ffd_weight_ref,
    wide,
    rel_ref,
    lane_ref,
    found_ref,
    points,
    cell_rows,
    cell_feat,
    base_feat,
    k_hi,
    k_lo,
    l_hi,
    l_lo,
    sens_rows,
    sens_slots,
    sens_mat,
    grad_slots,
    load_sem,
    halo_send,
    halo_recv,
    point_send,
    point_recv,
    sens_send,
    sens_recv,
    grad_send,
    grad_recv,
    known,
    met,
):
    cells, subs, nodes = (lax.axis_size(a) for a in ("cells", "sub", "nodes"))
    cell_at, sub_at, node_at = (lax.axis_index(a) for a in ("cells", "sub", "nodes"))
    here, places = cell_at * subs + sub_at, cells * subs
    team, crew = node_at * subs + sub_at, nodes * subs
    me, everyone = cell_at * crew + team, cells * crew
    nodes_here = weight_ref.shape[0]
    rows = adj_hbm.shape[1]
    blocks = rows // nodes_here
    cell_count = blocks * LANES
    base_own = base_ref.shape[1]
    panels = base_own // LANES

    lower, upper = cell_at > 0, cell_at < cells - 1
    below, above = cell_at - 1, cell_at + 1
    beside_count = lower.astype(jnp.int32) + upper.astype(jnp.int32)

    adj_load = pltpu.make_async_copy(
        adj_hbm, wide.at[0, :, pl.ds(rows, rows), :], load_sem.at[0]
    )
    adj_load.start()
    barrier = pltpu.get_barrier_semaphore()

    def greet(device):
        pl.semaphore_signal(barrier, inc=1, device_id=device, device_id_type=MESH)

    first, last = sub_at == 0, sub_at == subs - 1
    down, up = jnp.logical_and(lower, first), jnp.logical_and(upper, last)
    abroad = [(last, {"nodes": (node_at + step) % nodes}) for step in range(1, nodes)]
    abroad += [(down, {"cells": below, "sub": subs - 1}), (up, {"cells": above, "sub": 0})]
    greeted = jnp.int32(subs - 1)
    for exists, device in abroad:
        pl.when(exists)(functools.partial(greet, device))
        greeted = greeted + exists.astype(jnp.int32)
    for step in range(1, subs):
        greet({"sub": (sub_at + step) % subs})

    base_start = pl.multiple_of(team * base_own, LANES)
    share = pl.ds(base_start, base_own)
    sources = (
        (0, adj_hbm, wide.at[0, :, pl.ds(rows, rows), :]),
        (1, point_hbm, point_ref),
        (2, base_hbm.at[:, share], base_ref),
        (3, nb_hbm, nb_ref),
        (4, off_hbm, off_ref),
        (5, rhs_hbm, rhs_ref),
        (5, inv_hbm, inv_ref),
        (6, sens_hbm, sens_ref),
        (7, ffd_index_hbm.at[:, share], ffd_index_ref),
        (7, ffd_weight_hbm.at[:, share], ffd_weight_ref),
        (8, weight_hbm, weight_ref),
    )
    for group, source, target in sources[1:]:
        pltpu.make_async_copy(source, target, load_sem.at[group]).start()

    def arrive(size, sem):
        pltpu.make_async_copy(size, size, sem).wait()

    sizes = [source[2] for source in sources if source[0] not in (5, 7)]
    sizes.insert(5, wide)
    sizes.insert(7, cell_feat.at[0 : 2 * ffd_index_ref.shape[0], 0:base_own])

    def load_wait(*groups):
        for group in groups:
            arrive(sizes[group], load_sem.at[group])

    def tell(stage):
        for exists, other in ((upper, above), (lower, below)):

            @pl.when(exists)
            def _():
                pl.semaphore_signal(
                    known.at[stage],
                    inc=1,
                    device_id={"cells": other},
                    device_id_type=MESH,
                )

    def hear(stage):
        pl.semaphore_wait(known.at[stage], beside_count)

    def meet(which, device):
        pl.semaphore_signal(met.at[which], inc=1, device_id=device, device_id_type=MESH)

    def announce():
        for exists, device in abroad:
            pl.when(exists)(functools.partial(meet, 0, device))

    def pass_on():
        expected = greeted - (subs - 1)

        @pl.when(expected > 0)
        def _():
            pl.semaphore_wait(met.at[0], expected)

        @pl.when(jnp.logical_or(first, last))
        def _():
            for step in range(1, subs):
                meet(1, {"sub": (sub_at + step) % subs})

    def crew_known():
        if subs > 1:
            others = (sub_at != 0).astype(jnp.int32) + (sub_at != subs - 1).astype(jnp.int32)
            pl.semaphore_wait(met.at[1], others)

    @pl.when(here == 0)
    def _():
        wide[:, :, 0:rows, :] = jnp.zeros((SWEEPS, 5, rows, LANES), jnp.float32)

    @pl.when(here == places - 1)
    def _():
        wide[:, :, 2 * rows : 3 * rows, :] = jnp.zeros((SWEEPS, 5, rows, LANES), jnp.float32)

    pieces, stride = rows // ROWS, ROWS // nodes_here

    def halo(sweep, side, top=0, tall=rows):
        mark = side * pieces + top // ROWS if sweep == 0 else 2 * pieces + side
        other = here + 1 if side == 0 else here - 1
        start = 0 if side == 0 else 2 * rows
        return pltpu.make_async_remote_copy(
            src_ref=wide.at[sweep, :, pl.ds(rows + top, tall), :],
            dst_ref=wide.at[sweep, :, pl.ds(start + top, tall), :],
            send_sem=halo_send.at[side],
            recv_sem=halo_recv.at[mark],
            device_id={"cells": other // subs, "sub": other % subs},
            device_id_type=MESH,
        )

    def halo_start(sweep, piece, side):
        @pl.when(here < places - 1 if side == 0 else here > 0)
        def _():
            halo(sweep, side, piece * ROWS, ROWS).start()

    def halo_arrive(sweep, side):
        if sweep == 0:
            for piece in range(pieces):
                halo(sweep, side, piece * ROWS, ROWS).wait_recv()
        else:
            halo(sweep, side).wait_recv()

    def halo_sent():
        both = wide.at[:, :, pl.ds(rows, rows), :]

        @pl.when(here < places - 1)
        def _():
            arrive(both, halo_send.at[0])

        @pl.when(here > 0)
        def _():
            arrive(both, halo_send.at[1])

    def point_copy(step):
        return pltpu.make_async_remote_copy(
            src_ref=point_ref,
            dst_ref=points.at[step],
            send_sem=point_send.at[step - 1],
            recv_sem=point_recv.at[step - 1],
            device_id={"sub": (sub_at + step) % subs},
            device_id_type=MESH,
        )

    load_wait(0, 1)
    pl.semaphore_wait(barrier, greeted)
    for piece in range(pieces):
        halo_start(0, pieces - 1 - piece, 0)
        halo_start(0, piece, 1)
    for step in range(1, subs):
        point_copy(step).start()
    announce()

    load_wait(2, 3)
    first_cell = here * cell_count
    for face in range(nb_ref.shape[0]):
        for block in range(blocks):
            entry = nb_ref[face : face + 1, block * LANES : (block + 1) * LANES]
            local = entry - first_cell + cell_count
            chunk = jnp.where(entry >= 0, (local >> 7) - block, -1)
            span = pl.ds(block * nodes_here, nodes_here)
            rel_ref[face, span, :] = jnp.broadcast_to(chunk, (nodes_here, LANES))
            lane_ref[face, span, :] = jnp.broadcast_to(local & (LANES - 1), (nodes_here, LANES))

    def features(xyz, own):
        one, two, three = split3(xyz)
        square = xyz[0:1] * xyz[0:1] + xyz[1:2] * xyz[1:2] + xyz[2:3] * xyz[2:3]
        pieces = [one, one, two, two, one, three] if own else [one, two, one, two, three, one]
        parts = split3(square)
        ones = jnp.ones_like(square)
        for slot, piece in enumerate(pieces):
            cell_feat[3 * slot : 3 * slot + 3, 0 : xyz.shape[1]] = piece if own else -2.0 * piece
        for slot in range(3):
            cell_feat[18 + slot : 19 + slot, 0 : xyz.shape[1]] = parts[slot] if own else ones
            cell_feat[21 + slot : 22 + slot, 0 : xyz.shape[1]] = ones if own else parts[slot]

    stretch = 4.0 / support_radius
    features((base_ref[...] - 0.5) * stretch, False)
    base_feat[...] = cell_feat[:, 0:base_own].astype(jnp.bfloat16)

    def build_features(step):
        xyz = point_ref[...] if step == 0 else points[step]
        features((xyz - 0.5) * stretch, True)
        cell_rows[step] = cell_feat[:, 0:cell_count].T.astype(jnp.bfloat16)

    width = 2 * LANES

    def build_kernel(step, begin, end):
        for left in range(begin, end, width):
            other = base_feat[:, left : left + width]
            for top in range(0, cell_count, PIECE):
                mine = cell_rows[step, top : top + PIECE, :]
                target = slice(step * cell_count + top, step * cell_count + top + PIECE)
                squared = jnp.dot(mine, other, preferred_element_type=jnp.float32)
                squared = jnp.maximum(squared, 1e-20)
                ratio = squared * lax.rsqrt(squared)
                inside = jnp.maximum(4.0 - ratio, 0.0)
                fourth = inside * inside
                value = (fourth * fourth) * (5.0 - inside)
                for side in range(2):
                    hi, lo = split2(value[:, side * LANES : (side + 1) * LANES])
                    k_hi[left // LANES + side, target, :] = hi
                    k_lo[left // LANES + side, target, :] = lo

    def build_lattice(panel):
        at = slice(panel * LANES, (panel + 1) * LANES)
        index, weight = ffd_index_ref[:, at], ffd_weight_ref[:, at]
        slots = index.shape[0]
        slot = lax.broadcasted_iota(jnp.int32, index.shape, 0)
        total, repeat = weight, jnp.zeros(index.shape, jnp.int32)
        for turn in range(1, slots):
            same = pltpu.roll(index, turn, 0) == index
            total = total + jnp.where(same, pltpu.roll(weight, turn, 0), 0.0)
            repeat = jnp.where(jnp.logical_and(same, slot >= turn), 1, repeat)
        index = jnp.where(repeat == 1, -1, index)
        hi = total.astype(jnp.bfloat16).astype(jnp.float32)
        lo = total - hi
        tall = (2 * ROWS, LANES)

        def spread(value, kind):
            return [jnp.broadcast_to(value[s : s + 1], tall).astype(kind) for s in range(slots)]

        index, hi, lo = spread(index, jnp.int16), spread(hi, jnp.bfloat16), spread(lo, jnp.bfloat16)
        row = lax.broadcasted_iota(jnp.int32, tall, 0).astype(jnp.int16)
        for column in range(0, FFD, LANES):
            rows_hi, rows_lo = [], []
            for top in range(column, column + LANES, 2 * ROWS):
                found_hi = found_lo = jnp.zeros(tall, jnp.bfloat16)
                here_row = row + jnp.int16(top)
                for s in range(slots):
                    match = index[s] == here_row
                    found_hi = jnp.where(match, hi[s], found_hi)
                    found_lo = jnp.where(match, lo[s], found_lo)
                rows_hi.append(found_hi)
                rows_lo.append(found_lo)
            l_hi[column // LANES, at, :] = jnp.concatenate(rows_hi, axis=0).T
            l_lo[column // LANES, at, :] = jnp.concatenate(rows_lo, axis=0).T

    zero = jnp.zeros((ROWS, LANES), jnp.float32)

    def arrives_late(piece, chunk, far_low, far_high):
        first_row = chunk + stride * piece
        last_row = first_row + stride - 1
        return (far_low and first_row < blocks) or (far_high and last_row >= 2 * blocks)

    def seek(sweep, face, piece, found, chunks):
        span = slice(piece * ROWS, (piece + 1) * ROWS)
        rel, lane = rel_ref[face, span, :], lane_ref[face, span, :]
        for chunk in chunks:
            match = rel == chunk
            at = (chunk + stride * piece) * nodes_here
            for comp in range(5):
                window = wide[sweep, comp, at : at + ROWS, :]
                taken = jnp.take_along_axis(window, lane, axis=1)
                found[comp] = jnp.where(match, taken, found[comp])
        return found

    def chunk_lists(piece, far):
        late = [c for c in range(2 * blocks + 1) if arrives_late(piece, c, *far)]
        return [c for c in range(2 * blocks + 1) if c not in late], late

    def relax_early(sweep, far):
        for face in range(off_ref.shape[0]):
            for piece in range(pieces):
                found = seek(sweep, face, piece, [zero] * 5, chunk_lists(piece, far)[0])
                for comp in range(5):
                    found_ref[face, piece, comp] = found[comp]

    def relax_late(sweep, far):
        for piece in range(pieces - 1, -1, -1) if far == (True, False) else range(pieces):
            if sweep == 0 and subs > 1:
                for side, exists in enumerate((here > 0, here < places - 1)):
                    if far[side]:
                        pl.when(exists)(halo(0, side, piece * ROWS, ROWS).wait_recv)
            span = slice(piece * ROWS, (piece + 1) * ROWS)
            coupled = [zero] * 5
            for face in range(off_ref.shape[0]):
                found = [found_ref[face, piece, comp] for comp in range(5)]
                found = seek(sweep, face, piece, found, chunk_lists(piece, far)[1])
                for a in range(5):
                    for b in range(5):
                        block = off_ref[face, 5 * a + b, span].astype(jnp.float32)
                        coupled[a] = coupled[a] + block * found[b]
            rest = [rhs_ref[b, span] - coupled[b] for b in range(5)]
            for a in range(5):
                total = inv_ref[5 * a, span] * rest[0]
                for b in range(1, 5):
                    total = total + inv_ref[5 * a + b, span] * rest[b]
                if sweep + 1 < SWEEPS:
                    at = rows + piece * ROWS
                    wide[sweep + 1, a, at : at + ROWS, :] = total
                else:
                    out_ref[a, span] = total
            if sweep + 1 < SWEEPS:
                for side in range(2):
                    halo_start(sweep + 1, piece, side)

    def by_side(work, sweep):
        for far in sorted({(s == 0, s == subs - 1) for s in range(subs)}):
            same = jnp.logical_and(
                (sub_at == 0) == far[0], (sub_at == subs - 1) == far[1]
            )
            pl.when(same)(functools.partial(work, sweep, far))

    def halo_near(sweep):
        @pl.when(sub_at > 0)
        def _():
            halo_arrive(sweep, 0)

        @pl.when(sub_at < subs - 1)
        def _():
            halo_arrive(sweep, 1)

    def halo_far(sweep):
        @pl.when(jnp.logical_and(sub_at == 0, here > 0))
        def _():
            halo_arrive(sweep, 0)

        @pl.when(jnp.logical_and(sub_at == subs - 1, here < places - 1))
        def _():
            halo_arrive(sweep, 1)

    panel_pairs = base_own // width
    second_cut, third_cut = ((panel_pairs * part // 4) * width for part in (2, 3))

    def early_with(step, begin, end):
        def work(sweep, far):
            build_kernel(step, begin, end)
            relax_early(sweep, far)

        return work

    build_features(0)
    build_kernel(0, 0, second_cut)
    halo_near(0)
    by_side(early_with(0, second_cut, third_cut), 0)
    pass_on()
    load_wait(4, 5)
    if subs == 1:
        halo_far(0)
    by_side(relax_late, 0)
    crew_known()
    tell(0)
    for step in range(1, subs):
        point_copy(step).wait_recv()
        build_features(step)
    build_kernel(0, third_cut, base_own)
    for step in range(1, subs - 1):
        build_kernel(step, 0, base_own)
    load_wait(6, 7, 8)
    halo_near(1)
    by_side(early_with(subs - 1, 0, second_cut if subs > 1 else 0), 1)
    halo_far(1)
    by_side(relax_late, 1)
    for k in range(3):
        total = out_ref[0] * sens_ref[k].astype(jnp.float32)
        for a in range(1, 5):
            total = total + out_ref[a] * sens_ref[3 * a + k].astype(jnp.float32)
        sens_rows[k] = total
    for k in range(3):
        total = weight_ref[0] * sens_rows[k, pl.ds(0, blocks, stride=nodes_here), :]
        for n in range(1, nodes_here):
            total = total + weight_ref[n] * sens_rows[k, pl.ds(n, blocks, stride=nodes_here), :]
        sens_slots[team, k] = total

    def sens_copy(node_step, sub_step):
        return pltpu.make_async_remote_copy(
            src_ref=sens_slots.at[team],
            dst_ref=sens_slots.at[team],
            send_sem=sens_send,
            recv_sem=sens_recv,
            device_id={
                "nodes": (node_at + node_step) % nodes,
                "sub": (sub_at + sub_step) % subs,
            },
            device_id_type=MESH,
        )

    crew_steps = [(n, s) for n in range(1, nodes) for s in range(subs)]
    crew_steps += [(0, s) for s in range(1, subs)]
    for node_step, sub_step in crew_steps:
        sens_copy(node_step, sub_step).start()
    if cells > 2:
        hear(0)
        tell(1)
    sens_mat[...] = jnp.zeros_like(sens_mat)
    if subs > 1:
        build_kernel(subs - 1, second_cut, base_own)
    for panel in range(panels):
        build_lattice(panel)
    for stage in range(2, cells - 1):
        hear(stage - 1)
        tell(stage)
    arrive(sens_slots.at[pl.ds(0, crew - 1)], sens_recv)
    for step in range(subs):
        whose = (sub_at - step + subs) % subs
        for k in range(3):
            total = sens_slots[whose, k]
            for n in range(1, nodes):
                total = total + sens_slots[n * subs + whose, k]
            hi = total.astype(jnp.bfloat16).astype(jnp.float32)
            lo = total - hi
            for block in range(blocks):
                at = step * cell_count + block * LANES
                sens_mat[k : k + 1, at : at + LANES] = hi[block : block + 1, :]
                sens_mat[ROWS + k : ROWS + k + 1, at : at + LANES] = lo[block : block + 1, :]

    left = sens_mat[...].astype(jnp.bfloat16)
    pieces_hi, pieces_lo = [], []
    for pair in range(0, panels, 2):
        product = jnp.zeros((2 * ROWS, 2 * LANES), jnp.float32)
        for table in (k_hi, k_lo):
            both = jnp.concatenate([table[pair], table[pair + 1]], axis=1)
            product = product + jnp.dot(left, both, preferred_element_type=jnp.float32)
        base_grad = (product[0:ROWS] + product[ROWS:]) * scale
        hi = base_grad.astype(jnp.bfloat16).astype(jnp.float32)
        pieces_hi.append(hi)
        pieces_lo.append(base_grad - hi)
    left = jnp.concatenate(
        [jnp.concatenate(pieces_hi, axis=1), jnp.concatenate(pieces_lo, axis=1)], axis=0
    ).astype(jnp.bfloat16)
    owns = []
    for pair in range(0, FFD // LANES, 2):
        product = jnp.zeros((2 * ROWS, 2 * LANES), jnp.float32)
        for table in (l_hi, l_lo):
            both = jnp.concatenate([table[pair], table[pair + 1]], axis=1)
            product = product + jnp.dot(left, both, preferred_element_type=jnp.float32)
        owns.append(product[0:ROWS] + product[ROWS:])
    own = jnp.concatenate(owns, axis=1)
    for block in range(FFD // LANES):
        grad_slots[me, 3 * block : 3 * block + 3, :] = own[
            0:3, block * LANES : (block + 1) * LANES
        ]

    def grad_copy(slot):
        return pltpu.make_async_remote_copy(
            src_ref=grad_slots.at[me],
            dst_ref=grad_slots.at[me],
            send_sem=grad_send,
            recv_sem=grad_recv,
            device_id={
                "cells": slot // crew,
                "nodes": slot % crew // subs,
                "sub": slot % subs,
            },
            device_id_type=MESH,
        )

    if cells > 1:
        hear(cells - 2)
    for slot in range(everyone):
        pl.when(slot != me)(grad_copy(slot).start)
    halo_sent()
    for step in range(1, subs):
        point_copy(step).wait_send()
    arrive(sens_slots.at[pl.ds(0, crew - 1)], sens_send)
    others = grad_slots.at[pl.ds(0, everyone - 1)]
    arrive(others, grad_send)
    arrive(others, grad_recv)
    total = grad_slots[0]
    for slot in range(1, everyone):
        total = total + grad_slots[slot]
    for block in range(FFD // LANES):
        grad_ref[:, block * LANES : (block + 1) * LANES] = total[3 * block : 3 * block + 3, :]


def finish(adjoint_in, control_in, adjoint_out, control_out):
    adjoint_out[...] = adjoint_in[...]
    control_out[...] = control_in[...]


def to_rows(array):
    array = jnp.moveaxis(array, 0, -2)
    lead, (nodes, cells) = array.shape[:-2], array.shape[-2:]
    array = array.reshape(lead + (nodes, cells // LANES, LANES))
    array = jnp.swapaxes(array, -3, -2)
    return array.reshape(lead + (nodes * cells // LANES, LANES))


def from_rows(array, nodes):
    lead, rows = array.shape[:-2], array.shape[-2]
    array = array.reshape(lead + (rows // nodes, nodes, LANES))
    array = jnp.swapaxes(array, -3, -2).reshape(lead + (nodes, rows // nodes * LANES))
    return jnp.moveaxis(array, -2, 0)


def body(
    adjoint_start,
    adjoint_rhs,
    off_blocks,
    diag_inverse,
    neighbours,
    node_weights,
    sens_blocks,
    cell_points,
    base_points,
    ffd_index,
    ffd_weight,
):
    nodes_here, _, cell_count = adjoint_start.shape
    faces = off_blocks.shape[1]
    cells, subs, nodes = (lax.axis_size(a) for a in ("cells", "sub", "nodes"))
    crew = nodes * subs
    everyone = cells * crew
    blocks = cell_count // LANES
    rows = blocks * nodes_here
    base_own = base_points.shape[1] // crew
    panels = base_own // LANES
    scale = 1.0 / 256.0 / float(cell_count * cells * subs) ** 0.5
    vmem = pl.BlockSpec(memory_space=pltpu.VMEM)
    hbm = pl.BlockSpec(memory_space=pltpu.HBM)
    f32, bf16 = jnp.float32, jnp.bfloat16
    dma = pltpu.SemaphoreType.DMA
    off_rows, inv_rows = to_rows(off_blocks), to_rows(diag_inverse)
    sens_cells = to_rows(sens_blocks)
    adjoint, control = pl.pallas_call(
        functools.partial(kernel, scale),
        out_shape=(
            jax.ShapeDtypeStruct((5, rows, LANES), f32),
            jax.ShapeDtypeStruct((3, FFD), f32),
        ),
        in_specs=[hbm] * 11,
        out_specs=(vmem, vmem),
        scratch_shapes=[
            pltpu.SMEM(node_weights.shape, f32),
            pltpu.VMEM(cell_points.shape, f32),
            pltpu.VMEM(neighbours.shape, jnp.int32),
            pltpu.VMEM((3, base_own), f32),
            pltpu.VMEM(off_rows.shape, bf16),
            pltpu.VMEM((5, rows, LANES), f32),
            pltpu.VMEM(inv_rows.shape, f32),
            pltpu.VMEM(sens_cells.shape, bf16),
            pltpu.VMEM((ffd_index.shape[1], base_own), jnp.int32),
            pltpu.VMEM((ffd_index.shape[1], base_own), f32),
            pltpu.VMEM((SWEEPS, 5, 3 * rows, LANES), f32),
            pltpu.VMEM((faces, rows, LANES), jnp.int32),
            pltpu.VMEM((faces, rows, LANES), jnp.int32),
            pltpu.VMEM((faces, rows // ROWS, 5, ROWS, LANES), f32),
            pltpu.VMEM((subs, 3, cell_count), f32),
            pltpu.VMEM((subs, cell_count, 24), bf16),
            pltpu.VMEM((24, max(cell_count, base_own)), f32),
            pltpu.VMEM((24, base_own), bf16),
            pltpu.VMEM((panels, subs * cell_count, LANES), bf16),
            pltpu.VMEM((panels, subs * cell_count, LANES), bf16),
            pltpu.VMEM((FFD // LANES, base_own, LANES), bf16),
            pltpu.VMEM((FFD // LANES, base_own, LANES), bf16),
            pltpu.VMEM((3, rows, LANES), f32),
            pltpu.VMEM((crew, 3, blocks, LANES), f32),
            pltpu.VMEM((2 * ROWS, subs * cell_count), f32),
            pltpu.VMEM((everyone, 3 * FFD // LANES, LANES), f32),
            dma((9,)),
            dma((2,)),
            dma((2 * (rows // ROWS) + 2,)),
            dma((max(subs - 1, 1),)),
            dma((max(subs - 1, 1),)),
            dma,
            dma,
            dma,
            dma,
            pltpu.SemaphoreType.REGULAR((max(cells - 1, 1),)),
            pltpu.SemaphoreType.REGULAR((2,)),
        ],
        compiler_params=pltpu.CompilerParams(
            collective_id=0, has_side_effects=True, vmem_limit_bytes=16 * 1024 * 1024
        ),
    )(
        *(pltpu.with_memory_space_constraint(array, pltpu.HBM) for array in (
            node_weights,
            to_rows(adjoint_start),
            cell_points,
            neighbours,
            base_points,
            off_rows,
            to_rows(adjoint_rhs),
            inv_rows,
            sens_cells,
            ffd_index.T,
            ffd_weight.T,
        ))
    )
    adjoint, control = pl.pallas_call(
        finish,
        out_shape=(
            jax.ShapeDtypeStruct((5, rows, LANES), f32),
            jax.ShapeDtypeStruct((3, FFD), f32),
        ),
        in_specs=[vmem] * 2,
        out_specs=(vmem, vmem),
        compiler_params=pltpu.CompilerParams(vmem_limit_bytes=1024 * 1024),
    )(adjoint, control)
    return from_rows(adjoint, nodes_here), control


def solution(mesh):
    return jax.shard_map(
        body,
        mesh=mesh,
        in_specs=(
            P("nodes", None, ("groups", "cells", "sub")),
            P("nodes", None, ("groups", "cells", "sub")),
            P("nodes", None, None, ("groups", "cells", "sub")),
            P("nodes", None, ("groups", "cells", "sub")),
            P(None, ("cells", "sub")),
            P("nodes"),
            P("nodes", None, ("groups", "cells", "sub")),
            P(None, ("cells", "sub")),
            P(),
            P(),
            P(),
        ),
        out_specs=(P("nodes", None, ("groups", "cells", "sub")), P("groups", None)),
        check_vma=False,
    )
```
